128 devices in a mesh: grp: 4 (over x), seq: 32 (over z, y, core).
Axes of the slice: x: 4, y: 4, z: 4, core: 2. Of those that a mesh axis runs over, the one named last changes fastest.
Arguments:
- tokens: bfloat16 [24576, 2048], P(('grp', 'seq')), may hold values from -6 to 6
- w_query: bfloat16 [2048, 1024], replicated, may hold values from -0.125 to 0.125
- w_key: bfloat16 [2048, 1024], replicated, may hold values from -0.0078125 to 0.0078125
- w_value: bfloat16 [2048, 2048], replicated, may hold values from -0.125 to 0.125
- w_gate_down: bfloat16 [2048, 16], replicated, may hold values from -0.125 to 0.125
- w_gate_up: float32 [16, 1024], replicated, may hold values from -1.5 to 1.5
- gate_bias: float32 [1024], replicated, may hold values from -1.5 to 9
- norm_gain: bfloat16 [2048], replicated, may hold values from 0.25 to 1.75
- lengths: int32 [64], replicated, may hold values from 1 to 8192, 24576 in all
- owner: int32 [64], replicated, may hold values from 0 to 63, each once
Outputs:
- head_outputs: bfloat16 [24576, 2048], P(('grp', 'seq'))
- final_states: float32 [64, 2048, 256], P('grp', 'seq')
The draws below stay inside these ranges and needn't reach their ends.
Inputs may be any that keep to these rules, and one draw needn't show every extreme that they name: `lengths`: lengths sum to 24576; the longest is exactly 8192. `owner`: every row of final_states belongs to exactly one request.
All inputs are finite; a program needn't handle non-finite values.
Results may differ from the reference program's by a relative error of at most 0.0067.
Values may be sent and summed in bfloat16 or wider, within the bound.
No kernel may reach another device: no remote copies, remote signals or barrier semaphores. Data moves between devices by JAX's collectives and lax.ppermute only.
A program may use at most 192 MiB of HBM per device.

```python
import math
import jax
import jax.numpy as jnp
import numpy as np
from jax import lax

D = 2048
H = 4
HEAD_K = 256
VAL = 512
RANK = 16
SPAN = 64
REQS = 64
TOKENS = 24576
LONGEST = 8192


def shard_levels(own_key, extent, cuts, smallest, top_value):
    factor_of = 1.0
    for axis_at, parts in cuts:
        steps = jax.random.uniform(jax.random.fold_in(jax.random.fold_in(own_key, 6), axis_at), (parts,), jnp.float32, smallest / len(cuts), top_value / len(cuts))
        factor_of = factor_of * jnp.repeat(jnp.exp(steps), extent[axis_at] // parts).reshape((-1,) + (1,) * (len(extent) - 1 - axis_at))
    return factor_of


def length_profile(number_of, total, most, slope):
    portions = [(1 << 20) // math.isqrt(standing ** slope) + 1 for standing in range(2, number_of + 1)]
    rest, given = total - most - (number_of - 1), [1] * (number_of - 1)
    while rest > 0:
        movable = [i for i in range(number_of - 1) if given[i] < most]
        mass, budget = sum([portions[i] for i in movable]), rest
        for i in movable:
            more = min(most - given[i], max(1, budget * portions[i] // mass), rest)
            given[i] = given[i] + more
            rest = rest - more
    return np.array([most] + given)


def ragged(stream_key, count, total, limit, slope):
    if count == 2:
        one = jax.random.randint(stream_key, (), max(1, total - limit), min(limit, total - 1) + 1)
        return jnp.stack([one, total - one])
    tallies = jnp.asarray(length_profile(count, total, limit, slope), jnp.int32)
    pairs = (count - 1) // 2
    source_of, receiver = tallies[1:1 + 2 * pairs:2], tallies[2:2 + 2 * pairs:2]
    slack = jnp.minimum(source_of - 1, limit - receiver)
    shifted = jax.random.randint(jax.random.fold_in(stream_key, 1), (pairs,), 0, 1 << 20) % (slack + 1)
    tallies = tallies.at[1:1 + 2 * pairs:2].set(source_of - shifted).at[2:2 + 2 * pairs:2].set(receiver + shifted)
    return tallies[jax.random.permutation(jax.random.fold_in(stream_key, 2), count)]


def gaussian(key, extent, deviation, bound, shards=(), kind=jnp.bfloat16):
    result = jax.random.normal(key, extent, jnp.float32) * deviation
    if len(shards) > 0:
        result = shard_levels(key, extent, shards, -0.22, 0.18) * result
    return jnp.clip(result, min=-bound, max=bound).astype(kind)


def setup_inputs(seed: int = 0) -> dict:
    key_of = jax.random.split(jax.random.key(seed), 11)
    tokens = gaussian(key_of[0], (TOKENS, D), 1.0, 6.0, ((0, 128),))
    w_query = gaussian(key_of[1], (D, H * HEAD_K), D ** -0.5, 0.125)
    w_key = gaussian(key_of[2], (D, H * HEAD_K), (D * HEAD_K) ** -0.5, 0.0078125)
    w_value = gaussian(key_of[3], (D, H * VAL), D ** -0.5, 0.125)
    w_gate_down = gaussian(key_of[4], (D, RANK), D ** -0.5, 0.125)
    w_gate_up = gaussian(key_of[5], (RANK, H * HEAD_K), RANK ** -0.5, 1.5, (), jnp.float32)
    gate_bias = jnp.clip(jax.random.uniform(key_of[6], (H * HEAD_K,), jnp.float32, -1.5, 9.0), -1.5, 9.0)
    norm_gain = jnp.clip(1.0 + 0.15 * jax.random.normal(key_of[7], (H * VAL,), jnp.float32), 0.25, 1.75).astype(jnp.bfloat16)
    lengths = ragged(key_of[8], REQS, TOKENS, LONGEST, 2).astype(jnp.int32)
    owner = jax.random.permutation(key_of[9], REQS).astype(jnp.int32)
    return {"tokens": tokens, "w_query": w_query, "w_key": w_key, "w_value": w_value, "w_gate_down": w_gate_down, "w_gate_up": w_gate_up, "gate_bias": gate_bias, "norm_gain": norm_gain, "lengths": lengths, "owner": owner}


def segment_of(positions, starts):
    return lax.optimization_barrier(jnp.sum((starts[None, :] <= positions[:, None]).astype(jnp.int32), axis=1)).astype(jnp.int32) - 1

def block_terms(queries, key_rows, value_rows, log_gate, segments, seg_in):
    highest = lax.Precision.HIGHEST
    cumulative = jnp.cumsum(log_gate, axis=1)
    middle = cumulative[:, SPAN // 2 - 1:SPAN // 2, :]
    query_f = queries.astype(jnp.float32) * HEAD_K ** (-0.5)
    keys_f = key_rows.astype(jnp.float32)
    values_f = value_rows.astype(jnp.float32)
    query_rel = query_f * jnp.exp(cumulative - middle)
    key_rel = keys_f * jnp.exp(middle - cumulative)
    scores = jnp.einsum('nck,ndk->ncd', query_rel, key_rel, precision=highest)
    causal = jnp.arange(SPAN)[:, None] >= jnp.arange(SPAN)[None, :]
    same_seg = segments[:, :, None] == segments[:, None, :]
    masked = jnp.where(causal[None] & same_seg, scores, 0.0)
    within = jnp.einsum('ncd,ndv->ncv', masked, values_f, precision=highest)
    block_last = cumulative[:, -1:, :]
    keep_mask = (segments == segments[:, -1:])[:, :, None]
    key_end = keys_f * jnp.exp(block_last - cumulative) * keep_mask
    update = jnp.einsum('ndv,ndk->nvk', values_f, key_end, precision=highest)
    carry_decay = jnp.exp(block_last[:, 0, :]) * (segments[:, -1] == seg_in)[:, None]
    query_in = query_f * jnp.exp(cumulative) * (segments == seg_in[:, None])[:, :, None]
    return (within, query_in, update, carry_decay, cumulative, keys_f, values_f)

def end_states(keys_f, values_f, cumulative, segments, seg_in, state_in, block_id, offset, req_ids):
    highest = lax.Precision.HIGHEST
    chosen_keys = keys_f[block_id]
    chosen_values = values_f[block_id]
    chosen_cum = cumulative[block_id]
    chosen_seg = segments[block_id]
    positions = jnp.arange(SPAN, dtype=jnp.int32)
    at_end = positions[None, :, None] == offset[:, None, None]
    end_cum = lax.optimization_barrier(jnp.sum(jnp.where(at_end, chosen_cum, 0.0), axis=1, keepdims=True))
    live_mask = (positions[None, :] <= offset[:, None]) & (chosen_seg == req_ids[:, None])
    weighted = chosen_keys * jnp.exp(jnp.where(live_mask[:, :, None], end_cum - chosen_cum, 0.0)) * live_mask[:, :, None]
    end_piece = jnp.einsum('rcv,rck->rvk', chosen_values, weighted, precision=highest)
    enters = seg_in[block_id] == req_ids
    return end_piece + (jnp.exp(end_cum[:, 0, :]) * enters[:, None])[:, None, :] * state_in[block_id]

def reference(tokens, w_query, w_key, w_value, w_gate_down, w_gate_up, gate_bias, norm_gain, lengths, owner):
    highest = lax.Precision.HIGHEST
    queries = jnp.dot(tokens, w_query, preferred_element_type=jnp.float32).astype(jnp.bfloat16)
    key_rows = jnp.dot(tokens, w_key, preferred_element_type=jnp.float32).astype(jnp.bfloat16)
    value_rows = jnp.dot(tokens, w_value, preferred_element_type=jnp.float32).astype(jnp.bfloat16)
    lowrank = jnp.dot(tokens, w_gate_down, preferred_element_type=jnp.float32)
    log_gate = jax.nn.log_sigmoid(jnp.dot(lowrank, w_gate_up, precision=highest) + gate_bias) / 16.0
    starts = (jnp.cumsum(lengths) - lengths).astype(jnp.int32)
    block_count = TOKENS // SPAN
    segments = segment_of(jnp.arange(TOKENS, dtype=jnp.int32), starts).reshape(block_count, SPAN)
    seg_in = segment_of(jnp.arange(block_count, dtype=jnp.int32) * SPAN - 1, starts)
    ends_at = (starts + lengths - 1).astype(jnp.int32)
    block_id = (ends_at // SPAN).astype(jnp.int32)
    offset = (ends_at % SPAN).astype(jnp.int32)
    req_ids = jnp.arange(REQS, dtype=jnp.int32)
    block_width = min(VAL, 128)
    outputs = []
    finals = []
    for head_index in range(H):
        key_lo = head_index * HEAD_K
        query_head = queries[:, key_lo:key_lo + HEAD_K].reshape(block_count, SPAN, HEAD_K)
        key_head = key_rows[:, key_lo:key_lo + HEAD_K].reshape(block_count, SPAN, HEAD_K)
        gate_head = log_gate[:, key_lo:key_lo + HEAD_K].reshape(block_count, SPAN, HEAD_K)
        for column_block in range(VAL // block_width):
            value_lo = head_index * VAL + column_block * block_width
            value_head = value_rows[:, value_lo:value_lo + block_width].reshape(block_count, SPAN, block_width)
            within, query_in, update, carry_decay, cumulative, keys_f, values_f = block_terms(query_head, key_head, value_head, gate_head, segments, seg_in)

            def advance(state, inputs):
                decay, change = inputs
                return (decay[None, :] * state + change, state)
            last_state, state_in = lax.scan(advance, jnp.zeros((block_width, HEAD_K), jnp.float32), (carry_decay, update))
            out_block = within + jnp.einsum('nck,nvk->ncv', query_in, state_in, precision=highest)
            outputs.append(out_block.reshape(TOKENS, block_width))
            finals.append(end_states(keys_f, values_f, cumulative, segments, seg_in, state_in, block_id, offset, req_ids))
    attended = jnp.concatenate(outputs, axis=1).astype(jnp.bfloat16)
    heads_view = attended.astype(jnp.float32).reshape(TOKENS, H, VAL)
    mean_square = lax.optimization_barrier(jnp.mean(heads_view * heads_view, axis=2, keepdims=True))
    normed = heads_view * lax.rsqrt(mean_square + 1e-05) * norm_gain.astype(jnp.float32).reshape(1, H, VAL)
    head_outputs = normed.reshape(TOKENS, H * VAL).astype(jnp.bfloat16)
    pieces = jnp.concatenate(finals, axis=1)
    final_states = jnp.zeros_like(pieces).at[owner].set(pieces)
    return (head_outputs, final_states)
```

```python
import functools

import jax
import jax.numpy as jnp
from jax import lax
from jax.experimental import pallas as pl
from jax.experimental.pallas import tpu as pltpu
from jax.sharding import Mesh
from jax.sharding import PartitionSpec as P

H = 4
HEAD_K = 256
VAL = 512
SPAN = 64
SLOTS = 6
ROWS = 16
F32 = jnp.float32
BF16 = jnp.bfloat16
AXES = ("grp", "chip", "core")


def split3(x):
    a = x.astype(BF16)
    r = x - a.astype(F32)
    b = r.astype(BF16)
    c = (r - b.astype(F32)).astype(BF16)
    return a, b, c


def project_kernel(
    meta,
    tok_a,
    tok_b,
    w_k,
    w_v,
    w_q,
    w_down,
    w_up,
    bias,
    seg_col,
    seg_row,
    q_o,
    k_o,
    v_o,
    cum_o,
    qin_o,
    khat_o,
    carry_o,
    tok_s,
    erev_s,
    efwd_s,
    khc_s,
):
    step = pl.program_id(0)
    rows = tok_a.shape[0]
    chunk = 2 * rows
    core = meta[0]
    width = 2 * HEAD_K

    @pl.when(step == 0)
    def _():
        tok_s[pl.ds(pl.multiple_of(core * rows, rows), rows), :] = tok_a[...]
        tok_s[pl.ds(pl.multiple_of((1 - core) * rows, rows), rows), :] = tok_b[...]
        low = jnp.dot(tok_s[...], w_down[...], preferred_element_type=F32)
        logit = (
            jnp.dot(low, w_up[...], precision=lax.Precision.HIGHEST, preferred_element_type=F32)
            + bias[...]
        )
        gate = (jnp.minimum(logit, 0.0) - jnp.log1p(jnp.exp(-jnp.abs(logit)))) / 16.0
        parts = split3(gate)
        low_tri = (
            lax.broadcasted_iota(jnp.int32, (SPAN, SPAN), 0)
            >= lax.broadcasted_iota(jnp.int32, (SPAN, SPAN), 1)
        ).astype(BF16)
        before = jnp.zeros((1, width), F32)
        for b in range(chunk // SPAN):
            at = slice(b * SPAN, (b + 1) * SPAN)
            cum = sum(
                jnp.dot(low_tri, part[at, :], preferred_element_type=F32) for part in parts[::-1]
            )
            cum_o[at, :] = cum
            efwd_s[at, :] = jnp.exp(before + cum)
            before = before + cum[SPAN - 1 : SPAN, :]
        later = (
            (
                lax.broadcasted_iota(jnp.int32, (chunk, chunk), 0)
                < lax.broadcasted_iota(jnp.int32, (chunk, chunk), 1)
            )
            & (seg_col[...] == seg_row[...])
        ).astype(F32).astype(BF16)
        erev_s[...] = jnp.exp(
            sum(jnp.dot(later, part, preferred_element_type=F32) for part in parts[::-1])
        )
        row = lax.broadcasted_iota(jnp.int32, (chunk, 1), 0)
        tail = jnp.sum(jnp.where(row == meta[3], efwd_s[...], 0.0), axis=0, keepdims=True)
        whole = jnp.where(meta[2] == 1, efwd_s[chunk - 1 : chunk, :], 0.0)
        eight = lax.broadcasted_iota(jnp.int32, (8, width), 0)
        whole_hi = whole.astype(BF16).astype(F32)
        tail_hi = tail.astype(BF16).astype(F32)
        packed = jnp.where(
            eight == 0,
            whole_hi,
            jnp.where(
                eight == 1,
                whole - whole_hi,
                jnp.where(eight == 2, tail_hi, jnp.where(eight == 3, tail - tail_hi, 0.0)),
            ),
        ).astype(BF16)
        for h in range(2):
            piece = packed[:, h * HEAD_K : (h + 1) * HEAD_K]
            carry_o[:, 8 * h : 8 * h + 8, ROWS : ROWS + 8, :] = jnp.broadcast_to(
                piece[None, None], (4, 8, 8, HEAD_K)
            )

    @pl.when(step < 2)
    def _():
        cols = pl.ds(pl.multiple_of(step * HEAD_K, HEAD_K), HEAD_K)
        keys = jnp.dot(tok_s[...], w_k[...], preferred_element_type=F32).astype(BF16)
        k_o[:, cols] = keys
        khat = keys.astype(F32) * erev_s[:, cols]
        khat_o[:, cols] = khat.astype(BF16)
        khc_s[:, cols] = jnp.where(seg_col[...] == meta[1], khat, 0.0).astype(BF16)

    @pl.when((step >= 2) & (step < 6))
    def _():
        part = step - 2
        values = jnp.dot(tok_s[...], w_v[...], preferred_element_type=F32)
        v_o[:, pl.ds(pl.multiple_of(part * HEAD_K, HEAD_K), HEAD_K)] = values.astype(BF16)
        keys = khc_s[:, pl.ds(pl.multiple_of((part // 2) * HEAD_K, HEAD_K), HEAD_K)]
        piece = jnp.dot(values.T.astype(BF16), keys, preferred_element_type=F32)
        piece = piece.astype(BF16).reshape(4, 4, ROWS, HEAD_K)
        for g in range(4):
            carry_o[g, pl.ds(4 * part, 4), 0:ROWS, :] = piece[:, g]

    @pl.when(step >= 6)
    def _():
        cols = pl.ds(pl.multiple_of((step - 6) * HEAD_K, HEAD_K), HEAD_K)
        queries = jnp.dot(tok_s[...], w_q[...], preferred_element_type=F32).astype(BF16)
        q_o[:, cols] = queries
        entering = queries.astype(F32) * (HEAD_K**-0.5) * efwd_s[:, cols]
        qin_o[:, cols] = jnp.where(seg_col[...] == meta[4], entering, 0.0).astype(BF16)


def project(meta, tok_a, tok_b, w_key, w_value, w_query, w_down, w_up, bias, seg_col, seg_row):
    rows, depth = tok_a.shape
    chunk = 2 * rows
    rank = w_down.shape[1]
    whole = lambda *shape: pl.BlockSpec(shape, lambda i, m: (0,) * len(shape))
    return pl.pallas_call(
        project_kernel,
        grid_spec=pltpu.PrefetchScalarGridSpec(
            num_scalar_prefetch=1,
            grid=(8,),
            in_specs=[
                whole(rows, depth),
                whole(rows, depth),
                pl.BlockSpec((depth, HEAD_K), lambda i, m: (0, 2 * m[0] + jnp.clip(i, 0, 1))),
                pl.BlockSpec((depth, HEAD_K), lambda i, m: (0, 4 * m[0] + jnp.clip(i - 2, 0, 3))),
                pl.BlockSpec((depth, HEAD_K), lambda i, m: (0, 2 * m[0] + jnp.clip(i - 6, 0, 1))),
                whole(depth, rank),
                pl.BlockSpec((rank, 2 * HEAD_K), lambda i, m: (0, m[0])),
                pl.BlockSpec((1, 2 * HEAD_K), lambda i, m: (0, m[0])),
                whole(chunk, 1),
                whole(1, chunk),
            ],
            out_specs=[
                whole(chunk, 2 * HEAD_K),
                whole(chunk, 2 * HEAD_K),
                whole(chunk, 2 * VAL),
                whole(chunk, 2 * HEAD_K),
                whole(chunk, 2 * HEAD_K),
                whole(chunk, 2 * HEAD_K),
                whole(4, 16, ROWS + 8, HEAD_K),
            ],
            scratch_shapes=[
                pltpu.VMEM((chunk, depth), BF16),
                pltpu.VMEM((chunk, 2 * HEAD_K), F32),
                pltpu.VMEM((chunk, 2 * HEAD_K), F32),
                pltpu.VMEM((chunk, 2 * HEAD_K), BF16),
            ],
        ),
        out_shape=[
            jax.ShapeDtypeStruct((chunk, 2 * HEAD_K), BF16),
            jax.ShapeDtypeStruct((chunk, 2 * HEAD_K), BF16),
            jax.ShapeDtypeStruct((chunk, 2 * VAL), BF16),
            jax.ShapeDtypeStruct((chunk, 2 * HEAD_K), F32),
            jax.ShapeDtypeStruct((chunk, 2 * HEAD_K), BF16),
            jax.ShapeDtypeStruct((chunk, 2 * HEAD_K), BF16),
            jax.ShapeDtypeStruct((4, 16, ROWS + 8, HEAD_K), BF16),
        ],
        cost_estimate=pl.CostEstimate(
            flops=2 * chunk * depth * 2048, bytes_accessed=12 << 20, transcendentals=0
        ),
        name="project",
    )(meta, tok_a, tok_b, w_key, w_value, w_query, w_down, w_up, bias, seg_col, seg_row)


def pieces_kernel(first, v_ref, khat_ref, seg_col, out_ref):
    for h in range(2):
        turned = v_ref[:, h * VAL : (h + 1) * VAL].astype(F32).T.astype(BF16)
        keys = khat_ref[:, h * HEAD_K : (h + 1) * HEAD_K].astype(F32)
        for j in range(SLOTS):
            live = jnp.where(seg_col[...] == first[0] + j, keys, 0.0).astype(BF16)
            piece = jnp.dot(turned, live, preferred_element_type=F32)
            piece = piece.astype(BF16).reshape(8, 4, ROWS, HEAD_K)
            for g in range(4):
                out_ref[g, 8 * h : 8 * h + 8, ROWS * j : ROWS * (j + 1), :] = piece[:, g]


def end_pieces(first, values, khat, seg_col):
    chunk = values.shape[0]
    return pl.pallas_call(
        pieces_kernel,
        in_specs=[pl.BlockSpec(memory_space=pltpu.SMEM)]
        + [pl.BlockSpec(memory_space=pltpu.VMEM)] * 3,
        out_specs=pl.BlockSpec(memory_space=pltpu.VMEM),
        out_shape=jax.ShapeDtypeStruct((4, 16, SLOTS * ROWS, HEAD_K), BF16),
        cost_estimate=pl.CostEstimate(
            flops=4 * SLOTS * chunk * VAL * HEAD_K, bytes_accessed=5 << 20, transcendentals=0
        ),
        name="end_pieces",
    )(first, values, khat, seg_col)


def within_kernel(q_ref, k_ref, v_ref, cum_ref, seg_col, seg_row, out_ref, far_s):
    chunk = q_ref.shape[0]
    causal = lax.broadcasted_iota(jnp.int32, (SPAN, SPAN), 0) >= lax.broadcasted_iota(
        jnp.int32, (SPAN, SPAN), 1
    )
    nt = (((1,), (1,)), ((), ()))
    for h in range(2):
        cols = slice(h * HEAD_K, (h + 1) * HEAD_K)
        vals = slice(h * VAL, (h + 1) * VAL)
        far_s[...] = jnp.zeros_like(far_s)
        for b in range(chunk // SPAN):
            at = slice(b * SPAN, (b + 1) * SPAN)
            cum = cum_ref[at, cols]
            middle = cum[SPAN // 2 - 1 : SPAN // 2, :]
            last = cum[SPAN - 1 : SPAN, :]
            query = q_ref[at, cols].astype(F32) * (HEAD_K**-0.5)
            key = k_ref[at, cols].astype(F32)
            scores = lax.dot_general(
                (query * jnp.exp(cum - middle)).astype(BF16),
                (key * jnp.exp(middle - cum)).astype(BF16),
                nt,
                preferred_element_type=F32,
            )
            same = seg_col[at, :] == seg_row[:, at]
            near = jnp.where(causal & same, scores, 0.0).astype(BF16)
            total = jnp.dot(near, v_ref[at, vals], preferred_element_type=F32)
            if b > 0:
                reach = 2 * SPAN * ((b + 1) // 2)
                scores = lax.dot_general(
                    (query * jnp.exp(cum)).astype(BF16),
                    far_s[0:reach, :].astype(BF16),
                    nt,
                    preferred_element_type=F32,
                )
                same = seg_col[at, :] == seg_row[:, 0:reach]
                far = jnp.where(same, scores, 0.0).astype(BF16)
                total += jnp.dot(far, v_ref[0:reach, vals], preferred_element_type=F32)
                far_s[0 : b * SPAN, :] = far_s[0 : b * SPAN, :] * jnp.exp(last)
            far_s[at, :] = key * jnp.exp(last - cum)
            out_ref[at, vals] = total


def within(q, k, v, cum, seg_col, seg_row):
    chunk = q.shape[0]
    return pl.pallas_call(
        within_kernel,
        in_specs=[pl.BlockSpec(memory_space=pltpu.VMEM)] * 6,
        out_specs=pl.BlockSpec(memory_space=pltpu.VMEM),
        out_shape=jax.ShapeDtypeStruct((chunk, 2 * VAL), F32),
        scratch_shapes=[pltpu.VMEM((chunk, HEAD_K), F32)],
        cost_estimate=pl.CostEstimate(
            flops=2 * chunk * chunk * (HEAD_K + VAL) * 2, bytes_accessed=5 << 20, transcendentals=0
        ),
        name="within",
    )(q, k, v, cum, seg_col, seg_row)


def scan_kernel(got, enter_o, keep_o):
    def body(c, state):
        enter_o[c] = state.astype(BF16)
        keep_o[c] = state
        decay = got[c, ROWS : ROWS + 8, :].astype(F32)
        carry = got[c, 0:ROWS, :].astype(F32)
        return (decay[0:1, :] + decay[1:2, :]) * state + carry

    lax.fori_loop(0, got.shape[0], body, jnp.zeros((ROWS, HEAD_K), F32))


def scan_chips(got):
    chips = got.shape[0]
    return pl.pallas_call(
        scan_kernel,
        in_specs=[pl.BlockSpec(memory_space=pltpu.VMEM)],
        out_specs=[pl.BlockSpec(memory_space=pltpu.VMEM)] * 2,
        out_shape=[
            jax.ShapeDtypeStruct((chips, ROWS, HEAD_K), BF16),
            jax.ShapeDtypeStruct((chips, ROWS, HEAD_K), F32),
        ],
        cost_estimate=pl.CostEstimate(flops=1 << 20, bytes_accessed=3 << 20, transcendentals=0),
        name="scan_chips",
    )(got)


def finals_kernel(base, info, ends, keep, got, old, out_ref):
    out_ref[...] = old[...]

    def body(r, unused):
        chip = info[r]
        slot = info[64 + r] - base[0]
        enters = info[128 + r].astype(F32)
        where_to = info[192 + r]

        @pl.when((slot >= 0) & (slot < SLOTS))
        def _():
            decay = got[chip, ROWS : ROWS + 8, :].astype(F32)
            decay = (decay[2:3, :] + decay[3:4, :]) * enters
            piece = ends[chip, pl.ds(pl.multiple_of(slot * ROWS, ROWS), ROWS), :].astype(F32)
            out_ref[where_to] = (piece + decay * keep[chip]).astype(BF16)

        return unused

    lax.fori_loop(0, info.shape[0] // 4, body, 0)


def finals(base, info, ends, keep, got, old):
    return pl.pallas_call(
        finals_kernel,
        in_specs=[pl.BlockSpec(memory_space=pltpu.SMEM)] * 2
        + [pl.BlockSpec(memory_space=pltpu.VMEM)] * 4,
        out_specs=pl.BlockSpec(memory_space=pltpu.VMEM),
        out_shape=jax.ShapeDtypeStruct(old.shape, BF16),
        cost_estimate=pl.CostEstimate(flops=1 << 20, bytes_accessed=5 << 20, transcendentals=0),
        name="finals",
    )(base, info, ends, keep, got, old)


def output_kernel(core, within_ref, qin_ref, enter_ref, gain_ref, mine_o, other_o):
    rows = mine_o.shape[0]
    nt = (((1,), (1,)), ((), ()))
    for h in range(2):
        state = jnp.stack([enter_ref[g, 8 * h : 8 * h + 8] for g in range(4)], axis=1)
        state = state.reshape(VAL, HEAD_K)
        gain = gain_ref[:, h * VAL : (h + 1) * VAL].astype(F32)
        for side, out in ((core[0], mine_o), (1 - core[0], other_o)):
            at = pl.ds(pl.multiple_of(side * rows, rows), rows)
            o = within_ref[at, h * VAL : (h + 1) * VAL] + lax.dot_general(
                qin_ref[at, h * HEAD_K : (h + 1) * HEAD_K], state, nt, preferred_element_type=F32
            )
            mean = jnp.mean(o * o, axis=1, keepdims=True)
            out[:, h * VAL : (h + 1) * VAL] = (o * lax.rsqrt(mean + 1e-05) * gain).astype(BF16)


def outputs(core, inner, qin, enter, gain):
    chunk = inner.shape[0]
    half = jax.ShapeDtypeStruct((chunk // 2, 2 * VAL), BF16)
    return pl.pallas_call(
        output_kernel,
        grid_spec=pltpu.PrefetchScalarGridSpec(
            num_scalar_prefetch=1,
            grid=(1,),
            in_specs=[
                pl.BlockSpec(inner.shape, lambda i, m: (0, 0)),
                pl.BlockSpec(qin.shape, lambda i, m: (0, 0)),
                pl.BlockSpec(enter.shape, lambda i, m: (0, 0, 0, 0)),
                pl.BlockSpec((1, 2 * VAL), lambda i, m: (0, m[0])),
            ],
            out_specs=[pl.BlockSpec(half.shape, lambda i, m: (0, 0))] * 2,
        ),
        out_shape=[half, half],
        cost_estimate=pl.CostEstimate(
            flops=4 * chunk * VAL * HEAD_K, bytes_accessed=4 << 20, transcendentals=0
        ),
        name="outputs",
    )(core, inner, qin, enter, gain)


def join_kernel(core, mine, other, out):
    width = mine.shape[1]
    out[:, pl.ds(pl.multiple_of(core[0] * width, width), width)] = mine[...]
    out[:, pl.ds(pl.multiple_of((1 - core[0]) * width, width), width)] = other[...]


def join(core, mine, other):
    return pl.pallas_call(
        join_kernel,
        in_specs=[pl.BlockSpec(memory_space=pltpu.SMEM)]
        + [pl.BlockSpec(memory_space=pltpu.VMEM)] * 2,
        out_specs=pl.BlockSpec(memory_space=pltpu.VMEM),
        out_shape=jax.ShapeDtypeStruct((mine.shape[0], 2 * mine.shape[1]), BF16),
        name="join",
    )(core, mine, other)


def gather_kernel(grp, a, b, c, d, out):
    for shift, piece in enumerate((a, b, c, d)):
        at = lax.rem(grp[0] + 4 - shift, 4)
        out[:, pl.ds(pl.multiple_of(at * ROWS, ROWS), ROWS), :] = piece[...].astype(F32)


def gather_finals(grp, pieces):
    reqs = pieces[0].shape[0]
    return pl.pallas_call(
        gather_kernel,
        in_specs=[pl.BlockSpec(memory_space=pltpu.SMEM)]
        + [pl.BlockSpec(memory_space=pltpu.VMEM)] * 4,
        out_specs=pl.BlockSpec(memory_space=pltpu.VMEM),
        out_shape=jax.ShapeDtypeStruct((reqs, 4 * ROWS, HEAD_K), F32),
        name="gather_finals",
    )(grp, *pieces)


def owner_route(shift):
    pairs = []
    for g in range(4):
        for t in range(16):
            for p in range(2):
                dest = ((g + shift) % 4) * 32 + 16 * p + t
                pairs.append((g * 32 + 2 * t + p, dest))
    return pairs


def on_device(
    tokens, w_query, w_key, w_value, w_gate_down, w_gate_up, gate_bias, norm_gain, lengths, owner
):
    core = lax.axis_index("core")
    grp = lax.axis_index("grp")
    chip = grp * 16 + lax.axis_index("chip")
    rows = tokens.shape[0]
    chunk = 2 * rows
    reqs = lengths.shape[0]
    other = lax.ppermute(tokens, "core", [(0, 1), (1, 0)])
    ids = jnp.arange(reqs, dtype=jnp.int32)
    ends = jnp.sum(jnp.where(ids[None, :] <= ids[:, None], lengths[None, :], 0), axis=1)
    begins = ends - lengths
    base = chip * chunk
    at = base + jnp.arange(chunk, dtype=jnp.int32)
    segs = jnp.sum((ends[None, :] <= at[:, None]).astype(jnp.int32), axis=1)
    marks = jnp.stack([base, base + chunk - 1, base - 1, base + chunk])
    marks = jnp.sum((ends[None, :] <= marks[:, None]).astype(jnp.int32), axis=1)
    first, last, before = marks[0], marks[1], marks[2]
    first_end = jnp.sum(jnp.where(ids == first, ends, 0)) - 1 - base
    meta = jnp.stack(
        [
            core,
            last,
            (before == last).astype(jnp.int32),
            jnp.clip(first_end, 0, chunk - 1),
            before,
        ]
    )
    req_chip = (ends - 1) // chunk
    seen = jnp.sum((ends[None, :] <= (req_chip * chunk)[:, None]).astype(jnp.int32), axis=1)
    slot = ids - seen
    enters = (begins < req_chip * chunk).astype(jnp.int32)
    where_to = ((owner // 16 + 4 - grp) % 4) * 16 + owner % 16
    info = jnp.concatenate([req_chip, slot, enters, where_to])
    seg_col = segs.reshape(chunk, 1)
    seg_row = segs.reshape(1, chunk)
    q, k, v, cum, qin, khat, carry = project(
        meta,
        tokens,
        other,
        w_key,
        w_value,
        w_query,
        w_gate_down,
        w_gate_up,
        gate_bias.reshape(1, -1),
        seg_col,
        seg_row,
    )
    chips = ("grp", "chip")
    got = lax.all_to_all(
        carry.reshape(64, ROWS + 8, HEAD_K), chips, split_axis=0, concat_axis=0, tiled=True
    )
    piece = end_pieces(first.reshape(1), v, khat, seg_col)
    ends_got = lax.all_to_all(
        piece.reshape(64, SLOTS * ROWS, HEAD_K), chips, split_axis=0, concat_axis=0, tiled=True
    )
    inner = within(q, k, v, cum, seg_col, seg_row)
    enter, keep = scan_chips(got)
    enter_here = lax.all_to_all(enter, chips, split_axis=0, concat_axis=0, tiled=True)
    mine, theirs = outputs(
        core.reshape(1), inner, qin, enter_here.reshape(4, 16, ROWS, HEAD_K), norm_gain.reshape(1, -1)
    )
    swapped = lax.ppermute(theirs, "core", [(0, 1), (1, 0)])
    head_outputs = join(core.reshape(1), mine, swapped)

    zero = jnp.zeros((reqs, ROWS, HEAD_K), BF16)
    result = finals(jnp.zeros((1,), jnp.int32), info, ends_got, keep, got, zero)
    most = jnp.max(slot)

    def more(state):
        return state[0] <= most

    def another(state):
        start, held = state
        extra = end_pieces((first + start).reshape(1), v, khat, seg_col)
        extra = lax.all_to_all(
            extra.reshape(64, SLOTS * ROWS, HEAD_K), chips, split_axis=0, concat_axis=0, tiled=True
        )
        return start + SLOTS, finals(start.reshape(1), info, extra, keep, got, held)

    _, result = lax.while_loop(more, another, (jnp.int32(SLOTS), result))
    result = result.reshape(4, reqs // 4, ROWS, HEAD_K)
    moved = [lax.ppermute(result[shift], AXES, owner_route(shift)) for shift in range(4)]
    final_states = gather_finals(grp.reshape(1), moved)
    return (head_outputs, final_states)


def solution(mesh):
    inner = Mesh(mesh.devices.reshape(4, 16, 2), AXES)
    spread = P(AXES, None)
    return jax.shard_map(
        on_device,
        mesh=inner,
        in_specs=(spread, P(), P(), P(), P(), P(), P(), P(), P(), P()),
        out_specs=(spread, P("grp", ("chip", "core"), None)),
        check_vma=False,
    )
```

```python
import jax
import jax.numpy as jnp
from jax import lax
from jax.experimental import pallas as pl
from jax.experimental.pallas import tpu as pltpu
from jax.sharding import Mesh
from jax.sharding import PartitionSpec as P

H = 4
HEAD_K = 256
VAL = 512
SPAN = 64
SLOTS = 6
MORE_SLOTS = 4
ROWS = 16
HEAD = ROWS + 8
F32 = jnp.float32
BF16 = jnp.bfloat16
AXES = ("grp", "chip", "core")
NT = (((1,), (1,)), ((), ()))


def iota(shape, axis):
    return lax.broadcasted_iota(jnp.int32, shape, axis)


def split3(x):
    a = x.astype(BF16)
    r = x - a.astype(F32)
    b = r.astype(BF16)
    return a, b, (r - b.astype(F32)).astype(BF16)


def holder_order(inverse):
    row = iota((VAL, VAL), 1 if inverse else 0)
    col = iota((VAL, VAL), 0 if inverse else 1)
    sub = row & 7
    value = 64 * (2 * (sub & 3) + (sub >> 2)) + (row >> 3)
    return jnp.where(col == value, 1.0, 0.0).astype(BF16)


def write_pieces(turned, keys, seg_col, first, out_ref, row, slots):
    for j in range(slots):
        live = jnp.where(seg_col == first + float(j), keys, 0.0).astype(BF16)
        piece = jnp.dot(turned, live, preferred_element_type=F32)
        at = pl.ds(pl.multiple_of(row + ROWS * j, 8), 8)
        out_ref[:, at, :] = piece.reshape(64, 8, HEAD_K).astype(BF16)


def project_kernel(
    dev,
    tok_a,
    tok_b,
    w_k,
    w_v,
    w_down,
    w_up,
    bias,
    lens,
    k_o,
    v_o,
    cum_o,
    khat_o,
    col_o,
    row_o,
    msg_o,
    tok_s,
    erev_s,
    order_s,
):
    step = pl.program_id(0)
    rows = tok_a.shape[0]
    chunk = 2 * rows
    core = dev[0] & 1
    width = 2 * HEAD_K
    reqs = lens.shape[1]
    blocks = chunk // SPAN

    @pl.when(step == 0)
    def _():
        tok_s[pl.ds(pl.multiple_of(core * rows, rows), rows), :] = tok_a[...]
        tok_s[pl.ds(pl.multiple_of((1 - core) * rows, rows), rows), :] = tok_b[...]
        order_s[...] = holder_order(False)
        base = ((dev[0] >> 1) * chunk).astype(F32)
        down, across = iota((reqs, reqs), 0), iota((reqs, reqs), 1)
        lens_f = lens[...].astype(F32)
        lens_col = jnp.sum(jnp.where(down == across, lens_f, 0.0), axis=1, keepdims=True)
        ends_col = jnp.sum(jnp.where(across <= down, lens_f, 0.0), axis=1, keepdims=True)
        ends_row = jnp.sum(jnp.where(down <= across, lens_col, 0.0), axis=0, keepdims=True)
        pos_col = base + iota((chunk, 1), 0).astype(F32)
        pos_row = base + iota((1, chunk), 1).astype(F32)
        seg_col = jnp.sum(jnp.where(ends_row <= pos_col, 1.0, 0.0), axis=1, keepdims=True)
        seg_row = jnp.sum(jnp.where(ends_col <= pos_row, 1.0, 0.0), axis=0, keepdims=True)
        before = jnp.sum(jnp.where(ends_row < base, 1.0, 0.0), axis=1, keepdims=True)
        first, last = seg_col[0:1, :], seg_col[chunk - 1 : chunk, :]
        ids = iota((1, reqs), 1).astype(F32)
        first_end = jnp.sum(jnp.where(ids == first, ends_row, 0.0), axis=1, keepdims=True) - 1.0
        col_o[...] = seg_col
        row_o[...] = seg_row

        six = jnp.concatenate([w_down[...]] * 6, axis=0)
        low = lax.dot_general(tok_s[...], six, NT, preferred_element_type=F32)
        l1, l2, l3 = split3(low)
        rank = w_down.shape[0]
        lane = iota(low.shape, 1)
        low = jnp.where(
            lane < 3 * rank,
            l1.astype(F32),
            jnp.where(lane < 5 * rank, l2.astype(F32), l3.astype(F32)),
        ).astype(BF16)
        u1, u2, u3 = split3(w_up[...])
        ups = jnp.concatenate([u1, u2, u3, u1, u2, u1], axis=0)
        logit = jnp.dot(low, ups, preferred_element_type=F32) + bias[...]
        gate = (jnp.minimum(logit, 0.0) - jnp.log1p(jnp.exp(-jnp.abs(logit)))) / 16.0
        parts = split3(gate)
        b_row, b_col = iota((SPAN, SPAN), 0), iota((SPAN, SPAN), 1)
        low_tri = jnp.where(b_row >= b_col, 1.0, 0.0).astype(BF16)
        low_tri = jnp.concatenate([low_tri] * 3, axis=1)
        cums, sufs, tops = [], [], []
        for b in range(blocks):
            at = slice(b * SPAN, (b + 1) * SPAN)
            three = jnp.concatenate([part[at, :] for part in parts], axis=0)
            cum = jnp.dot(low_tri, three, preferred_element_type=F32)
            cum_o[at, :] = cum
            cums.append(cum)
            later = (b_row < b_col) & (seg_col[at, :] == seg_row[:, at])
            later = jnp.where(later, 1.0, 0.0).astype(BF16)
            later = jnp.concatenate([later] * 3, axis=1)
            sufs.append(jnp.dot(later, three, preferred_element_type=F32))
            tops.append(sufs[-1][0:1, :] + gate[b * SPAN : b * SPAN + 1, :])
        over = jnp.zeros((1, width), F32)
        for b in range(blocks - 1, -1, -1):
            at = slice(b * SPAN, (b + 1) * SPAN)
            if b < blocks - 1:
                next_seg = seg_col[(b + 1) * SPAN : (b + 1) * SPAN + 1, :]
                on = jnp.where(seg_col[at, :] == next_seg, over, 0.0)
                erev_s[at, :] = jnp.exp(sufs[b] + on)
                over = tops[b] + jnp.where(seg_col[b * SPAN : b * SPAN + 1, :] == next_seg, over, 0.0)
            else:
                erev_s[at, :] = jnp.exp(sufs[b])
                over = tops[b]
        decay = jnp.exp(over)
        whole = jnp.where(before == last, decay, 0.0)
        whole_hi = whole.astype(BF16).astype(F32)
        tail_hi = decay.astype(BF16).astype(F32)
        eight = iota((8, HEAD_K), 0)
        packed = jnp.zeros((8, HEAD_K), F32)
        for h in range(2):
            cols = slice(h * HEAD_K, (h + 1) * HEAD_K)
            for n, x in enumerate((whole_hi, whole - whole_hi, tail_hi, decay - tail_hi)):
                packed = jnp.where(eight == 4 * h + n, x[:, cols], packed)
        msg_o[:, ROWS:HEAD, :] = jnp.broadcast_to(packed.astype(BF16)[None], (64, 8, HEAD_K))

    @pl.when(step < 2)
    def _():
        cols = pl.ds(pl.multiple_of(step * HEAD_K, HEAD_K), HEAD_K)
        keys = jnp.dot(tok_s[...], w_k[...], preferred_element_type=F32).astype(BF16)
        k_o[:, cols] = keys
        khat_o[:, cols] = (keys.astype(F32) * erev_s[:, cols]).astype(BF16)

    @pl.when(step >= 2)
    def _():
        part = step - 2
        values = jnp.dot(tok_s[...], w_v[...], preferred_element_type=F32)
        v_o[:, pl.ds(pl.multiple_of(part * HEAD_K, HEAD_K), HEAD_K)] = values.astype(BF16)

    @pl.when((step == 3) | (step == 5))
    def _():
        h = (step - 3) // 2
        values = v_o[:, pl.ds(pl.multiple_of(h * VAL, VAL), VAL)]
        turned = lax.dot_general(order_s[...], values, NT, preferred_element_type=F32).astype(BF16)
        keys = khat_o[:, pl.ds(pl.multiple_of(h * HEAD_K, HEAD_K), HEAD_K)].astype(F32)
        seg_col = col_o[...]
        write_pieces(turned, keys, seg_col, seg_col[chunk - 1 : chunk, :], msg_o, 8 * h, 1)
        write_pieces(turned, keys, seg_col, seg_col[0:1, :], msg_o, HEAD + 8 * h, SLOTS)


def project(dev, tok_a, tok_b, w_key, w_value, w_down, w_up, bias, lens):
    rows, depth = tok_a.shape
    chunk = 2 * rows
    rank = w_down.shape[0]
    whole = lambda *shape: pl.BlockSpec(shape, lambda i, m: (0,) * len(shape))
    half = lambda: pl.BlockSpec((rank, 2 * HEAD_K), lambda i, m: (0, m[0] & 1))
    outs = [
        jax.ShapeDtypeStruct((chunk, 2 * HEAD_K), BF16),
        jax.ShapeDtypeStruct((chunk, 2 * VAL), BF16),
        jax.ShapeDtypeStruct((chunk, 2 * HEAD_K), F32),
        jax.ShapeDtypeStruct((chunk, 2 * HEAD_K), BF16),
        jax.ShapeDtypeStruct((chunk, 1), F32),
        jax.ShapeDtypeStruct((1, chunk), F32),
        jax.ShapeDtypeStruct((64, HEAD + SLOTS * ROWS, HEAD_K), BF16),
    ]
    return pl.pallas_call(
        project_kernel,
        grid_spec=pltpu.PrefetchScalarGridSpec(
            num_scalar_prefetch=1,
            grid=(6,),
            in_specs=[
                whole(rows, depth),
                whole(rows, depth),
                pl.BlockSpec((depth, HEAD_K), lambda i, m: (0, 2 * (m[0] & 1) + jnp.clip(i, 0, 1))),
                pl.BlockSpec(
                    (depth, HEAD_K), lambda i, m: (0, 4 * (m[0] & 1) + jnp.clip(i - 2, 0, 3))
                ),
                whole(rank, depth),
                half(),
                pl.BlockSpec((1, 2 * HEAD_K), lambda i, m: (0, m[0] & 1)),
                whole(1, lens.shape[1]),
            ],
            out_specs=[whole(*o.shape) for o in outs],
            scratch_shapes=[
                pltpu.VMEM((chunk, depth), BF16),
                pltpu.VMEM((chunk, 2 * HEAD_K), F32),
                pltpu.VMEM((VAL, VAL), BF16),
            ],
        ),
        out_shape=outs,
        cost_estimate=pl.CostEstimate(
            flops=2 * chunk * depth * 2048, bytes_accessed=12 << 20, transcendentals=0
        ),
        name="project",
    )(dev, tok_a, tok_b, w_key, w_value, w_down, w_up, bias, lens)


def pieces_kernel(start, v_ref, khat_ref, seg_col, out_ref):
    order = holder_order(False)
    first = seg_col[0:1, :] + start[0].astype(F32)
    for h in range(2):
        values = v_ref[:, h * VAL : (h + 1) * VAL]
        turned = lax.dot_general(order, values, NT, preferred_element_type=F32).astype(BF16)
        keys = khat_ref[:, h * HEAD_K : (h + 1) * HEAD_K].astype(F32)
        write_pieces(turned, keys, seg_col[...], first, out_ref, 8 * h, MORE_SLOTS)


def end_pieces(start, values, khat, seg_col):
    return pl.pallas_call(
        pieces_kernel,
        in_specs=[pl.BlockSpec(memory_space=pltpu.SMEM)]
        + [pl.BlockSpec(memory_space=pltpu.VMEM)] * 3,
        out_specs=pl.BlockSpec(memory_space=pltpu.VMEM),
        out_shape=jax.ShapeDtypeStruct((64, MORE_SLOTS * ROWS, HEAD_K), BF16),
        name="end_pieces",
    )(start, values, khat, seg_col)


def within_kernel(
    dev, tok_a, tok_b, w_q, k_ref, v_ref, cum_ref, seg_col, seg_row, lens, out_ref, qin_o, q_s, far_s
):
    rows = tok_a.shape[0]
    chunk = 2 * rows
    core = dev[0] & 1
    mine = pl.ds(pl.multiple_of(core * rows, rows), rows)
    theirs = pl.ds(pl.multiple_of((1 - core) * rows, rows), rows)
    q_s[mine, :] = jnp.dot(tok_a[...], w_q[...], preferred_element_type=F32)
    q_s[theirs, :] = jnp.dot(tok_b[...], w_q[...], preferred_element_type=F32)
    base = ((dev[0] >> 1) * chunk).astype(F32)
    reqs = lens.shape[1]
    down, across = iota((reqs, reqs), 0), iota((reqs, reqs), 1)
    ends_col = jnp.sum(
        jnp.where(across <= down, lens[...].astype(F32), 0.0), axis=1, keepdims=True
    )
    before = jnp.sum(jnp.where(ends_col < base, 1.0, 0.0), axis=0, keepdims=True)
    causal = iota((SPAN, SPAN), 0) >= iota((SPAN, SPAN), 1)
    far_s[...] = jnp.zeros_like(far_s)
    start = jnp.zeros((1, HEAD_K), F32)
    for b in range(chunk // SPAN):
        at = slice(b * SPAN, (b + 1) * SPAN)
        cum = cum_ref[at, :]
        middle = cum[SPAN // 2 - 1 : SPAN // 2, :]
        last = cum[SPAN - 1 : SPAN, :]
        query = q_s[at, :].astype(BF16).astype(F32) * (HEAD_K**-0.5)
        entering = query * jnp.exp(start + cum)
        qin_o[at, :] = jnp.where(seg_col[at, :] == before, entering, 0.0).astype(BF16)
        start = start + last
        key = k_ref[at, :].astype(F32)
        scores = lax.dot_general(
            (query * jnp.exp(cum - middle)).astype(BF16),
            (key * jnp.exp(middle - cum)).astype(BF16),
            NT,
            preferred_element_type=F32,
        )
        same = seg_col[at, :] == seg_row[:, at]
        near = jnp.where(causal & same, scores, 0.0).astype(BF16)
        total = jnp.dot(near, v_ref[at, :], preferred_element_type=F32)
        if b > 0:
            reach = 2 * SPAN * ((b + 1) // 2)
            scores = lax.dot_general(
                (query * jnp.exp(cum)).astype(BF16),
                far_s[0:reach, :].astype(BF16),
                NT,
                preferred_element_type=F32,
            )
            same = seg_col[at, :] == seg_row[:, 0:reach]
            far = jnp.where(same, scores, 0.0).astype(BF16)
            total += jnp.dot(far, v_ref[0:reach, :], preferred_element_type=F32)
            far_s[0 : b * SPAN, :] = far_s[0 : b * SPAN, :] * jnp.exp(last)
        far_s[at, :] = key * jnp.exp(last - cum)
        out_ref[at, :] = total


def within(dev, tok_a, tok_b, w_query, k, v, cum, seg_col, seg_row, lens):
    rows, depth = tok_a.shape
    chunk = 2 * rows
    whole = lambda *shape: pl.BlockSpec(shape, lambda i, m: (0,) * len(shape))
    head = lambda width: pl.BlockSpec((chunk, width), lambda i, m: (0, i))
    return pl.pallas_call(
        within_kernel,
        grid_spec=pltpu.PrefetchScalarGridSpec(
            num_scalar_prefetch=1,
            grid=(2,),
            in_specs=[
                whole(rows, depth),
                whole(rows, depth),
                pl.BlockSpec((depth, HEAD_K), lambda i, m: (0, 2 * (m[0] & 1) + i)),
                head(HEAD_K),
                head(VAL),
                head(HEAD_K),
                whole(chunk, 1),
                whole(1, chunk),
                whole(1, lens.shape[1]),
            ],
            out_specs=[head(VAL), head(HEAD_K)],
            scratch_shapes=[pltpu.VMEM((chunk, HEAD_K), F32)] * 2,
        ),
        out_shape=[
            jax.ShapeDtypeStruct((chunk, 2 * VAL), F32),
            jax.ShapeDtypeStruct((chunk, 2 * HEAD_K), BF16),
        ],
        cost_estimate=pl.CostEstimate(
            flops=2 * chunk * depth * 512 * 3, bytes_accessed=8 << 20, transcendentals=0
        ),
        name="within",
    )(dev, tok_a, tok_b, w_query, k, v, cum, seg_col, seg_row, lens)


COLLECTOR = (0, 1, 2, 3, 8, 9, 10, 11, 4, 5, 6, 7, 12, 13, 14, 15)


def scan_body(start, slots, row, info, got, ends, old, out_ref, keep_s, fin_s):
    chips = got.shape[0]
    reqs = info.shape[0] // 4
    each = reqs // 4

    def advance(c, state):
        out_ref[c, 0:ROWS, :] = state.astype(BF16)
        keep_s[c] = state
        decay = got[c, ROWS:HEAD, :].astype(F32)
        carry = got[c, 0:ROWS, :].astype(F32)
        return jnp.concatenate(
            [
                (decay[0:1, :] + decay[1:2, :]) * state[0:8, :] + carry[0:8, :],
                (decay[4:5, :] + decay[5:6, :]) * state[8:16, :] + carry[8:16, :],
            ],
            axis=0,
        )

    lax.fori_loop(0, chips, advance, jnp.zeros((ROWS, HEAD_K), F32), unroll=4)
    if old is not None:
        for g in range(4):
            for u in range(16):
                at = slice((g * 16 + u) * each, (g * 16 + u + 1) * each)
                held = old[g * 16 + COLLECTOR[u], ROWS : ROWS + each, :].astype(F32)
                for n, side in enumerate(fin_s):
                    side[at, :] = held[:, n * 128 : (n + 1) * 128]

    def finish(r, unused):
        chip = info[r]
        slot = info[reqs + r] - start
        enters = info[2 * reqs + r].astype(F32)
        owner = info[3 * reqs + r]

        @pl.when((slot >= 0) & (slot < slots))
        def _():
            decay = got[chip, ROWS:HEAD, :].astype(F32) * enters
            piece = ends[chip, pl.ds(pl.multiple_of(row + slot * ROWS, 8), ROWS), :].astype(F32)
            state = keep_s[chip]
            done = piece + jnp.concatenate(
                [
                    (decay[2:3, :] + decay[3:4, :]) * state[0:8, :],
                    (decay[6:7, :] + decay[7:8, :]) * state[8:16, :],
                ],
                axis=0,
            )
            first = (owner // each) * (16 * each) + owner % each
            for n, side in enumerate(fin_s):
                side[pl.ds(first, 16, stride=each), :] = done[:, n * 128 : (n + 1) * 128]

        return unused

    lax.fori_loop(0, reqs, finish, 0)
    for g in range(4):
        for u in range(16):
            at = slice((g * 16 + u) * each, (g * 16 + u + 1) * each)
            for n, side in enumerate(fin_s):
                cols = slice(n * 128, (n + 1) * 128)
                out_ref[g * 16 + COLLECTOR[u], ROWS : ROWS + each, cols] = side[at, :].astype(BF16)


def scan_kernel(info, got, out_ref, keep_s, *fin_s):
    scan_body(0, SLOTS, HEAD, info, got, got, None, out_ref, keep_s, fin_s)


def scan_more_kernel(start, info, got, ends, old, out_ref, keep_s, *fin_s):
    scan_body(start[0], MORE_SLOTS, 0, info, got, ends, old, out_ref, keep_s, fin_s)


def scan_chips(info, got, more=None):
    chips = got.shape[0]
    reqs = info.shape[0] // 4
    smem, vmem = pl.BlockSpec(memory_space=pltpu.SMEM), pl.BlockSpec(memory_space=pltpu.VMEM)
    if more is None:
        kernel, args, specs = scan_kernel, (info, got), [smem, vmem]
    else:
        start, ends, old = more
        kernel, args = scan_more_kernel, (start, info, got, ends, old)
        specs = [smem, smem, vmem, vmem, vmem]
    return pl.pallas_call(
        kernel,
        in_specs=specs,
        out_specs=vmem,
        out_shape=jax.ShapeDtypeStruct((chips, ROWS + reqs // 4, HEAD_K), BF16),
        scratch_shapes=[
            pltpu.VMEM((chips, ROWS, HEAD_K), F32),
            pltpu.VMEM((16 * reqs, 128), F32),
            pltpu.VMEM((16 * reqs, 128), F32),
        ],
        cost_estimate=pl.CostEstimate(flops=1 << 20, bytes_accessed=6 << 20, transcendentals=0),
        name="scan_chips",
    )(*args)


def collect_kernel(back, out_ref, *rows_s):
    reqs = out_ref.shape[0]
    for n, side in enumerate(rows_s):
        cols = slice(n * 128, (n + 1) * 128)
        side[...] = back[:, ROWS : ROWS + reqs, cols].astype(F32).reshape(64 * reqs, 128)
        for j in range(reqs):
            out_ref[j, :, cols] = side[pl.ds(j, 64, stride=reqs), :].astype(BF16)


def collect(back):
    reqs = back.shape[1] - ROWS
    return pl.pallas_call(
        collect_kernel,
        in_specs=[pl.BlockSpec(memory_space=pltpu.VMEM)],
        out_specs=pl.BlockSpec(memory_space=pltpu.VMEM),
        out_shape=jax.ShapeDtypeStruct((reqs, 64, HEAD_K), BF16),
        scratch_shapes=[pltpu.VMEM((64 * reqs, 128), F32)] * 2,
        cost_estimate=pl.CostEstimate(flops=1 << 16, bytes_accessed=2 << 20, transcendentals=0),
        name="collect",
    )(back)


def output_kernel(dev, within_ref, qin_ref, back, gain_ref, mine_o, other_o):
    rows = mine_o.shape[0]
    core = dev[0] & 1
    order = holder_order(True)
    for h in range(2):
        state = back[:, 8 * h : 8 * h + 8, :].astype(F32).reshape(VAL, HEAD_K).astype(BF16)
        state = jnp.dot(order, state, preferred_element_type=F32).astype(BF16)
        gain = gain_ref[:, h * VAL : (h + 1) * VAL].astype(F32)
        for side, out in ((1 - core, other_o), (core, mine_o)):
            at = pl.ds(pl.multiple_of(side * rows, rows), rows)
            o = within_ref[at, h * VAL : (h + 1) * VAL] + lax.dot_general(
                qin_ref[at, h * HEAD_K : (h + 1) * HEAD_K], state, NT, preferred_element_type=F32
            )
            mean = jnp.mean(o * o, axis=1, keepdims=True)
            out[:, h * VAL : (h + 1) * VAL] = (o * lax.rsqrt(mean + 1e-05) * gain).astype(BF16)


def outputs(dev, inner, qin, back, gain):
    chunk = inner.shape[0]
    half = jax.ShapeDtypeStruct((chunk // 2, 2 * VAL), BF16)
    return pl.pallas_call(
        output_kernel,
        grid_spec=pltpu.PrefetchScalarGridSpec(
            num_scalar_prefetch=1,
            grid=(1,),
            in_specs=[
                pl.BlockSpec(inner.shape, lambda i, m: (0, 0)),
                pl.BlockSpec(qin.shape, lambda i, m: (0, 0)),
                pl.BlockSpec(back.shape, lambda i, m: (0, 0, 0)),
                pl.BlockSpec((1, 2 * VAL), lambda i, m: (0, m[0] & 1)),
            ],
            out_specs=[pl.BlockSpec(half.shape, lambda i, m: (0, 0))] * 2,
        ),
        out_shape=[half, half],
        cost_estimate=pl.CostEstimate(
            flops=4 * chunk * VAL * HEAD_K, bytes_accessed=4 << 20, transcendentals=0
        ),
        name="outputs",
    )(dev, inner, qin, back, gain)


def join_kernel(dev, mine, other, out):
    width = mine.shape[1]
    core = dev[0] & 1
    out[:, pl.ds(pl.multiple_of(core * width, width), width)] = mine[...]
    out[:, pl.ds(pl.multiple_of((1 - core) * width, width), width)] = other[...]


def join(dev, mine, other):
    return pl.pallas_call(
        join_kernel,
        in_specs=[pl.BlockSpec(memory_space=pltpu.SMEM)]
        + [pl.BlockSpec(memory_space=pltpu.VMEM)] * 2,
        out_specs=pl.BlockSpec(memory_space=pltpu.VMEM),
        out_shape=jax.ShapeDtypeStruct((mine.shape[0], 2 * mine.shape[1]), BF16),
        name="join",
    )(dev, mine, other)


def home_route():
    pairs = []
    for t in range(16):
        for p in range(2):
            pairs.append((2 * t + p, 16 * p + 2 * (t % 8) + t // 8))
    return pairs


def exchange(x):
    return lax.all_to_all(x, ("grp", "chip"), split_axis=0, concat_axis=0, tiled=True)


def on_device(
    tokens, w_query, w_key, w_value, w_gate_down, w_gate_up, gate_bias, norm_gain, lengths, owner
):
    dev = lax.axis_index(AXES).astype(jnp.int32).reshape(1)
    chunk = 2 * tokens.shape[0]
    reqs = lengths.shape[0]
    other = lax.ppermute(tokens, "core", [(0, 1), (1, 0)])
    lens = lengths.reshape(1, reqs)
    k, v, cum, khat, seg_col, seg_row, msg = project(
        dev,
        tokens,
        other,
        w_key,
        w_value,
        w_gate_down.T,
        w_gate_up,
        gate_bias.reshape(1, -1),
        lens,
    )
    got = exchange(msg)
    inner, qin = within(dev, tokens, other, w_query, k, v, cum, seg_col, seg_row, lens)

    ids = jnp.arange(reqs, dtype=jnp.int32)
    ends = jnp.sum(jnp.where(ids[None, :] <= ids[:, None], lengths[None, :], 0), axis=1)
    req_chip = (ends - 1) // chunk
    seen = jnp.sum((ends[None, :] <= (req_chip * chunk)[:, None]).astype(jnp.int32), axis=1)
    slot = ids - seen
    enters = (ends - lengths < req_chip * chunk).astype(jnp.int32)
    info = jnp.concatenate([req_chip, slot, enters, owner])
    most = jnp.max(slot)
    done = scan_chips(info, got)

    def another(state):
        start, held = state
        extra = exchange(end_pieces(start.reshape(1), v, khat, seg_col))
        return start + MORE_SLOTS, scan_chips(info, got, (start.reshape(1), extra, held))

    _, done = lax.while_loop(lambda s: s[0] <= most, another, (jnp.int32(SLOTS), done))
    back = exchange(done)
    final = lax.ppermute(collect(back), ("chip", "core"), home_route())
    mine, theirs = outputs(dev, inner, qin, back, norm_gain.reshape(1, -1))
    swapped = lax.ppermute(theirs, "core", [(0, 1), (1, 0)])
    return (join(dev, mine, swapped), final.astype(F32))


def solution(mesh):
    inner = Mesh(mesh.devices.reshape(4, 16, 2), AXES)
    spread = P(AXES, None)
    return jax.shard_map(
        on_device,
        mesh=inner,
        in_specs=(spread, P(), P(), P(), P(), P(), P(), P(), P(), P()),
        out_specs=(spread, P("grp", ("chip", "core"), None)),
        check_vma=False,
    )
```

```python
import functools

import jax
import jax.numpy as jnp
from jax import lax
from jax.experimental import pallas as pl
from jax.experimental.pallas import tpu as pltpu
from jax.sharding import Mesh
from jax.sharding import PartitionSpec as P

H = 4
HEAD_K = 256
VAL = 512
SPAN = 64
SLOT_CHOICES = (4, 5, 6)
MORE_SLOTS = 4
ROWS = 16
HEAD = ROWS + 8
F32 = jnp.float32
BF16 = jnp.bfloat16
AXES = ("grp", "chip", "core")
NT = (((1,), (1,)), ((), ()))


def iota(shape, axis):
    return lax.broadcasted_iota(jnp.int32, shape, axis)


def split2(x):
    a = x.astype(BF16)
    return a, (x - a.astype(F32)).astype(BF16)


def split3(x):
    a = x.astype(BF16)
    r = x - a.astype(F32)
    b = r.astype(BF16)
    return a, b, (r - b.astype(F32)).astype(BF16)


def holder_order(inverse):
    row = iota((1, VAL), 1) if inverse else iota((VAL, 1), 0)
    sub = row & 7
    value = 64 * (2 * (sub & 3) + (sub >> 2)) + (row >> 3)
    col = iota((VAL, VAL), 0 if inverse else 1)
    return jnp.where(col == value, 1.0, 0.0).astype(BF16)


def ends_of(lens, down, across):
    lens_f = lens.astype(F32)
    lens_col = jnp.sum(jnp.where(down == across, lens_f, 0.0), axis=1, keepdims=True)
    ends_col = jnp.sum(jnp.where(across <= down, lens_f, 0.0), axis=1, keepdims=True)
    ends_row = jnp.sum(jnp.where(down <= across, lens_col, 0.0), axis=0, keepdims=True)
    return ends_col, ends_row


def plan_kernel(chunk, lens, owner, info_o, which_o):
    reqs = lens.shape[1]
    ends_col, ends = ends_of(lens[...], iota((reqs, reqs), 0), iota((reqs, reqs), 1))
    chip = jnp.floor((ends - 0.5) * (1.0 / chunk))
    seen = jnp.sum(jnp.where(ends_col <= chip * chunk, 1.0, 0.0), axis=0, keepdims=True)
    slot = iota((1, reqs), 1).astype(F32) - seen
    enters = jnp.where(ends - lens[...].astype(F32) < chip * chunk, 1, 0)
    at = iota((1, reqs), 1).astype(F32) * chunk
    first = jnp.sum(jnp.where(ends_col < at, 1.0, 0.0), axis=0, keepdims=True)
    last = jnp.sum(jnp.where(ends_col <= at + (chunk - 1.0), 1.0, 0.0), axis=0, keepdims=True)
    inside = jnp.where(first == last, 1, 0)
    rows = (chip.astype(jnp.int32), slot.astype(jnp.int32), enters, owner[...], inside)
    for n, row in enumerate(rows):
        info_o[n : n + 1, 0:reqs] = row
    most = jnp.max(slot, axis=1, keepdims=True) + 1.0
    which = sum(jnp.where(most > float(slots), 1, 0) for slots in SLOT_CHOICES)
    which_o[...] = jnp.concatenate([which, most.astype(jnp.int32)], axis=1)


def plan(chunk, lens, owner):
    vmem = pl.BlockSpec(memory_space=pltpu.VMEM)
    return pl.pallas_call(
        functools.partial(plan_kernel, chunk),
        in_specs=[vmem] * 2,
        out_specs=[vmem] * 2,
        out_shape=[
            jax.ShapeDtypeStruct((8, 128), jnp.int32),
            jax.ShapeDtypeStruct((1, 2), jnp.int32),
        ],
        name="plan",
    )(lens, owner)


def project_kernel(
    dev,
    tok_a,
    tok_b,
    w_k,
    w_v,
    w_q,
    w_down,
    w_up,
    bias,
    lens,
    k_o,
    v_o,
    q_o,
    khat_o,
    cum_o,
    col_o,
    row_o,
    decay_o,
    tok_s,
    erev_s,
    sems,
):
    step = pl.program_id(0)
    rows = tok_a.shape[0]
    chunk = 2 * rows
    core = dev[0] & 1
    width = 2 * HEAD_K
    reqs = lens.shape[1]
    blocks = chunk // SPAN

    @pl.when(step == 0)
    def _():
        mine = pl.ds(pl.multiple_of(core * rows, rows), rows)
        theirs = pl.ds(pl.multiple_of((1 - core) * rows, rows), rows)
        copy_a = pltpu.make_async_copy(tok_a, tok_s.at[mine, :], sems.at[0])
        copy_b = pltpu.make_async_copy(tok_b, tok_s.at[theirs, :], sems.at[1])
        copy_a.start()
        copy_b.start()
        base = ((dev[0] >> 1) * chunk).astype(F32)
        ends_col, ends_row = ends_of(lens[...], iota((reqs, reqs), 0), iota((reqs, reqs), 1))
        pos_col = base + iota((chunk, 1), 0).astype(F32)
        pos_row = base + iota((1, chunk), 1).astype(F32)
        seg_col = jnp.sum(jnp.where(ends_row <= pos_col, 1.0, 0.0), axis=1, keepdims=True)
        seg_row = jnp.sum(jnp.where(ends_col <= pos_row, 1.0, 0.0), axis=0, keepdims=True)
        before = jnp.sum(jnp.where(ends_row < base, 1.0, 0.0), axis=1, keepdims=True)
        seg_col, seg_row = seg_col - before, seg_row - before
        col_o[...] = seg_col
        row_o[...] = seg_row
        six = jnp.concatenate([w_down[...]] * 6, axis=0)
        u1, u2, u3 = split3(w_up[...])
        ups = jnp.concatenate([u1, u2, u3, u1, u2, u1], axis=0)
        copy_a.wait()
        copy_b.wait()
        low = lax.dot_general(tok_s[...], six, NT, preferred_element_type=F32)
        l1, l2, l3 = split3(low)
        rank = w_down.shape[0]
        lane = iota(low.shape, 1)
        low = jnp.where(
            lane < 3 * rank,
            l1.astype(F32),
            jnp.where(lane < 5 * rank, l2.astype(F32), l3.astype(F32)),
        ).astype(BF16)
        logit = jnp.dot(low, ups, preferred_element_type=F32) + bias[...]
        gate = (jnp.minimum(logit, 0.0) - jnp.log(1.0 + jnp.exp(-jnp.abs(logit)))) * (1.0 / 16.0)
        parts = split2(gate)
        b_row, b_col = iota((SPAN, SPAN), 0), iota((SPAN, SPAN), 1)
        low_tri = jnp.where(b_row >= b_col, 1.0, 0.0).astype(BF16)
        low_tri = jnp.concatenate([low_tri] * 2, axis=1)
        sufs, tops = [], []
        for b in range(blocks):
            at = slice(b * SPAN, (b + 1) * SPAN)
            pair = jnp.concatenate([part[at, :] for part in parts], axis=0)
            cum_o[at, :] = jnp.dot(low_tri, pair, preferred_element_type=F32)
            later = (b_row < b_col) & (seg_col[at, :] == seg_row[:, at])
            later = jnp.where(later, 1.0, 0.0).astype(BF16)
            later = jnp.concatenate([later] * 2, axis=1)
            sufs.append(jnp.dot(later, pair, preferred_element_type=F32))
            tops.append(sufs[-1][0:1, :] + gate[b * SPAN : b * SPAN + 1, :])
        over = jnp.zeros((1, width), F32)
        for b in range(blocks - 1, -1, -1):
            at = slice(b * SPAN, (b + 1) * SPAN)
            if b < blocks - 1:
                next_seg = seg_col[(b + 1) * SPAN : (b + 1) * SPAN + 1, :]
                on = jnp.where(seg_col[at, :] == next_seg, over, 0.0)
                erev_s[at, :] = jnp.exp(sufs[b] + on)
                over = tops[b] + jnp.where(seg_col[b * SPAN : b * SPAN + 1, :] == next_seg, over, 0.0)
            else:
                erev_s[at, :] = jnp.exp(sufs[b])
                over = tops[b]
        decay = jnp.exp(over)
        high = decay.astype(BF16).astype(F32)
        eight = iota((8, HEAD_K), 0)
        packed = jnp.zeros((8, HEAD_K), F32)
        for h in range(2):
            cols = slice(h * HEAD_K, (h + 1) * HEAD_K)
            for n, x in enumerate((high, decay - high)):
                packed = jnp.where(eight == 4 * h + n, x[:, cols], packed)
        decay_o[...] = packed

    @pl.when(step < 2)
    def _():
        cols = pl.ds(pl.multiple_of(step * HEAD_K, HEAD_K), HEAD_K)
        keys = jnp.dot(tok_s[...], w_k[...], preferred_element_type=F32).astype(BF16)
        k_o[...] = keys
        khat_o[...] = (keys.astype(F32) * erev_s[:, cols]).astype(BF16)

    @pl.when((step >= 2) & (step < 6))
    def _():
        v_o[...] = jnp.dot(tok_s[...], w_v[...], preferred_element_type=F32).astype(BF16)

    @pl.when(step >= 6)
    def _():
        q_o[...] = jnp.dot(tok_s[...], w_q[...], preferred_element_type=F32).astype(BF16)


def project(dev, tok_a, tok_b, w_key, w_value, w_query, w_down, w_up, bias, lens):
    rows, depth = tok_a.shape
    chunk = 2 * rows
    rank = w_down.shape[0]
    whole = lambda *shape: pl.BlockSpec(shape, lambda i, m: (0,) * len(shape))
    weight = lambda first, many: pl.BlockSpec(
        (depth, HEAD_K), lambda i, m: (0, many * (m[0] & 1) + jnp.clip(i - first, 0, many - 1))
    )
    result = lambda first, many: pl.BlockSpec(
        (chunk, HEAD_K), lambda i, m: (0, jnp.clip(i - first, 0, many - 1))
    )
    shape = jax.ShapeDtypeStruct
    return pl.pallas_call(
        project_kernel,
        grid_spec=pltpu.PrefetchScalarGridSpec(
            num_scalar_prefetch=1,
            grid=(8,),
            in_specs=[
                pl.BlockSpec(memory_space=pl.ANY),
                pl.BlockSpec(memory_space=pl.ANY),
                weight(0, 2),
                weight(2, 4),
                weight(6, 2),
                whole(rank, depth),
                pl.BlockSpec((rank, 2 * HEAD_K), lambda i, m: (0, m[0] & 1)),
                pl.BlockSpec((1, 2 * HEAD_K), lambda i, m: (0, m[0] & 1)),
                whole(1, lens.shape[1]),
            ],
            out_specs=[
                result(0, 2),
                result(2, 4),
                result(6, 2),
                result(0, 2),
                whole(chunk, 2 * HEAD_K),
                whole(chunk, 1),
                whole(1, chunk),
                whole(8, HEAD_K),
            ],
            scratch_shapes=[
                pltpu.VMEM((chunk, depth), BF16),
                pltpu.VMEM((chunk, 2 * HEAD_K), F32),
                pltpu.SemaphoreType.DMA((2,)),
            ],
        ),
        out_shape=[
            shape((chunk, 2 * HEAD_K), BF16),
            shape((chunk, 2 * VAL), BF16),
            shape((chunk, 2 * HEAD_K), BF16),
            shape((chunk, 2 * HEAD_K), BF16),
            shape((chunk, 2 * HEAD_K), F32),
            shape((chunk, 1), F32),
            shape((1, chunk), F32),
            shape((8, HEAD_K), F32),
        ],
        cost_estimate=pl.CostEstimate(
            flops=2 * chunk * depth * 2048, bytes_accessed=12 << 20, transcendentals=0
        ),
        name="project",
    )(dev, tok_a, tok_b, w_key, w_value, w_query, w_down, w_up, bias, lens)


def pieces_kernel(slots, start, v_ref, khat_ref, seg_col, decay, out_ref, msg_s, sems):
    order = holder_order(False)
    seg = seg_col[...]
    first, last = seg[0:1, :], seg[-1:, :]
    turned, keys = [], []
    for h in range(2):
        values = v_ref[:, h * VAL : (h + 1) * VAL]
        turned.append(
            lax.dot_general(order, values, NT, preferred_element_type=F32).astype(BF16)
        )
        keys.append(khat_ref[:, h * HEAD_K : (h + 1) * HEAD_K].astype(F32))
    copies = []

    def send(low, high):
        at = slice(low, high)
        copy = pltpu.make_async_copy(msg_s.at[:, at, :], out_ref.at[:, at, :], sems.at[len(copies)])
        copy.start()
        copies.append(copy)

    def write(row, which):
        for h in range(2):
            live = jnp.where(seg == which, keys[h], 0.0).astype(BF16)
            piece = jnp.dot(turned[h], live, preferred_element_type=F32)
            at = slice(row + 8 * h, row + 8 * h + 8)
            msg_s[:, at, :] = piece.reshape(64, 8, HEAD_K).astype(BF16)

    if start is None:
        row = HEAD
        write(0, last)
        msg_s[:, ROWS:HEAD, :] = jnp.broadcast_to(decay[...].astype(BF16)[None], (64, 8, HEAD_K))
        send(0, HEAD)
    else:
        row = 0
        first = first + start[0].astype(F32)
    for j in range(slots):
        write(row + ROWS * j, first + float(j))
        send(row + ROWS * j, row + ROWS * (j + 1))
    for copy in copies:
        copy.wait()


def first_pieces_kernel(slots, *refs):
    pieces_kernel(slots, None, *refs)


def more_pieces_kernel(slots, start, *refs):
    pieces_kernel(slots, start, *refs)


def pieces(slots, values, khat, seg_col, decay, start=None):
    vmem = pl.BlockSpec(memory_space=pltpu.VMEM)
    rows = ROWS * slots + (HEAD if start is None else 0)
    kernel = first_pieces_kernel if start is None else more_pieces_kernel
    lead = [] if start is None else [start]
    return pl.pallas_call(
        functools.partial(kernel, slots),
        in_specs=[pl.BlockSpec(memory_space=pltpu.SMEM)] * len(lead) + [vmem] * 4,
        out_specs=pl.BlockSpec(memory_space=pl.ANY),
        out_shape=jax.ShapeDtypeStruct((64, rows, HEAD_K), BF16),
        scratch_shapes=[
            pltpu.VMEM((64, rows, HEAD_K), BF16),
            pltpu.SemaphoreType.DMA((slots + 1,)),
        ],
        name="pieces",
    )(*lead, values, khat, seg_col, decay)


COLLECTOR = (0, 1, 2, 3, 8, 9, 10, 11, 4, 5, 6, 7, 12, 13, 14, 15)


def scan_body(start, slots, row, info, got, ends, old, out_ref, keep_s, fin_s):
    chips = got.shape[0]
    reqs = chips
    each = reqs // 4

    def scaled(c, flag, state):
        decay = got[c, ROWS:HEAD, :].astype(F32) * flag.astype(F32)
        return jnp.concatenate(
            [
                (decay[0:1, :] + decay[1:2, :]) * state[0:8, :],
                (decay[4:5, :] + decay[5:6, :]) * state[8:16, :],
            ],
            axis=0,
        )

    def advance(c, state):
        out_ref[c, 0:ROWS, :] = state.astype(BF16)
        keep_s[c] = state
        return scaled(c, info[4, c], state) + got[c, 0:ROWS, :].astype(F32)

    lax.fori_loop(0, chips, advance, jnp.zeros((ROWS, HEAD_K), F32), unroll=8)
    if old is not None:
        for g in range(4):
            for u in range(16):
                at = slice((g * 16 + u) * each, (g * 16 + u + 1) * each)
                held = old[g * 16 + COLLECTOR[u], ROWS : ROWS + each, :].astype(F32)
                for n, side in enumerate(fin_s):
                    side[at, :] = held[:, n * 128 : (n + 1) * 128]

    def place(r, slot):
        chip, owner = info[0, r], info[3, r]
        piece = ends[chip, pl.ds(pl.multiple_of(row + slot * ROWS, 8), ROWS), :].astype(F32)
        done = piece + scaled(chip, info[2, r], keep_s[chip])
        first = (owner // each) * (16 * each) + owner % each
        for n, side in enumerate(fin_s):
            side[pl.ds(first, 16, stride=each), :] = done[:, n * 128 : (n + 1) * 128]

    def finish(r, unused):
        slot = info[1, r] - start
        if slots is None:
            place(r, slot)
        else:

            @pl.when((slot >= 0) & (slot < slots))
            def _():
                place(r, slot)

        return unused

    lax.fori_loop(0, reqs, finish, 0, unroll=8 if slots is None else 1)
    for g in range(4):
        for u in range(16):
            at = slice((g * 16 + u) * each, (g * 16 + u + 1) * each)
            for n, side in enumerate(fin_s):
                cols = slice(n * 128, (n + 1) * 128)
                out_ref[g * 16 + COLLECTOR[u], ROWS : ROWS + each, cols] = side[at, :].astype(BF16)


def scan_kernel(slots, info, got, out_ref, keep_s, *fin_s):
    scan_body(0, slots, HEAD, info, got, got, None, out_ref, keep_s, fin_s)


def scan_more_kernel(start, info, got, ends, old, out_ref, keep_s, *fin_s):
    scan_body(start[0], MORE_SLOTS, 0, info, got, ends, old, out_ref, keep_s, fin_s)


def scan_chips(info, got, slots=None, more=None):
    chips = got.shape[0]
    smem, vmem = pl.BlockSpec(memory_space=pltpu.SMEM), pl.BlockSpec(memory_space=pltpu.VMEM)
    if more is None:
        kernel = functools.partial(scan_kernel, slots)
        args, specs = (info, got), [smem, vmem]
    else:
        start, ends, old = more
        kernel, args = scan_more_kernel, (start, info, got, ends, old)
        specs = [smem, smem, vmem, vmem, vmem]
    return pl.pallas_call(
        kernel,
        in_specs=specs,
        out_specs=vmem,
        out_shape=jax.ShapeDtypeStruct((chips, ROWS + chips // 4, HEAD_K), BF16),
        scratch_shapes=[
            pltpu.VMEM((chips, ROWS, HEAD_K), F32),
            pltpu.VMEM((16 * chips, 128), F32),
            pltpu.VMEM((16 * chips, 128), F32),
        ],
        cost_estimate=pl.CostEstimate(flops=1 << 20, bytes_accessed=6 << 20, transcendentals=0),
        name="scan_chips",
    )(*args)


def collect_kernel(back, out_ref, *rows_s):
    reqs = out_ref.shape[0]
    for n, side in enumerate(rows_s):
        cols = slice(n * 128, (n + 1) * 128)
        side[...] = back[:, :, cols].astype(F32).reshape(64 * reqs, 128)
        for j in range(reqs):
            out_ref[j, :, cols] = side[pl.ds(j, 64, stride=reqs), :].astype(BF16)


def collect(back):
    reqs = back.shape[1] - ROWS
    return pl.pallas_call(
        collect_kernel,
        grid=(1,),
        in_specs=[pl.BlockSpec((64, ROWS, HEAD_K), lambda i: (0, 1, 0))],
        out_specs=pl.BlockSpec((reqs, 64, HEAD_K), lambda i: (0, 0, 0)),
        out_shape=jax.ShapeDtypeStruct((reqs, 64, HEAD_K), BF16),
        scratch_shapes=[pltpu.VMEM((64 * reqs, 128), F32)] * 2,
        cost_estimate=pl.CostEstimate(flops=1 << 16, bytes_accessed=2 << 20, transcendentals=0),
        name="collect",
    )(back)


def attend_kernel(
    dev, q_ref, k_ref, v_ref, cum_ref, seg_col, seg_row, back, gain_ref, mine_o, other_o, far_s, qin_s, sum_s
):
    chunk = q_ref.shape[0]
    rows = chunk // 2
    core = dev[0] & 1
    h = pl.program_id(0)
    causal = iota((SPAN, SPAN), 0) >= iota((SPAN, SPAN), 1)
    far_s[...] = jnp.zeros_like(far_s)
    start = jnp.zeros((1, HEAD_K), F32)
    for b in range(chunk // SPAN):
        at = slice(b * SPAN, (b + 1) * SPAN)
        cum = cum_ref[at, :]
        middle = cum[SPAN // 2 - 1 : SPAN // 2, :]
        last = cum[SPAN - 1 : SPAN, :]
        query = q_ref[at, :].astype(F32) * (HEAD_K**-0.5)
        entering = query * jnp.exp(cum)
        qin_s[at, :] = jnp.where(seg_col[at, :] == 0.0, entering * jnp.exp(start), 0.0).astype(BF16)
        start = start + last
        key = k_ref[at, :].astype(F32)
        scores = lax.dot_general(
            (query * jnp.exp(cum - middle)).astype(BF16),
            (key * jnp.exp(middle - cum)).astype(BF16),
            NT,
            preferred_element_type=F32,
        )
        same = seg_col[at, :] == seg_row[:, at]
        near = jnp.where(causal & same, scores, 0.0).astype(BF16)
        total = jnp.dot(near, v_ref[at, :], preferred_element_type=F32)
        if b > 0:
            reach = 2 * SPAN * ((b + 1) // 2)
            scores = lax.dot_general(
                entering.astype(BF16),
                far_s[0:reach, :].astype(BF16),
                NT,
                preferred_element_type=F32,
            )
            same = seg_col[at, :] == seg_row[:, 0:reach]
            far = jnp.where(same, scores, 0.0).astype(BF16)
            total += jnp.dot(far, v_ref[0:reach, :], preferred_element_type=F32)
            far_s[0 : b * SPAN, :] = far_s[0 : b * SPAN, :] * jnp.exp(last)
        far_s[at, :] = key * jnp.exp(last - cum)
        sum_s[at, :] = total
    state = back[:, pl.ds(pl.multiple_of(8 * h, 8), 8), :].astype(F32)
    state = state.reshape(VAL, HEAD_K).astype(BF16)
    state = jnp.dot(holder_order(True), state, preferred_element_type=F32).astype(BF16)
    gain = gain_ref[...].astype(F32)
    for side, out in ((1 - core, other_o), (core, mine_o)):
        at = pl.ds(pl.multiple_of(side * rows, rows), rows)
        o = sum_s[at, :] + lax.dot_general(qin_s[at, :], state, NT, preferred_element_type=F32)
        mean = jnp.mean(o * o, axis=1, keepdims=True)
        out[...] = (o * lax.rsqrt(mean + 1e-05) * gain).astype(BF16)


def attend(dev, q, k, v, cum, seg_col, seg_row, back, gain):
    chunk = q.shape[0]
    rows = chunk // 2
    whole = lambda *shape: pl.BlockSpec(shape, lambda i, m: (0,) * len(shape))
    head = lambda width: pl.BlockSpec((chunk, width), lambda i, m: (0, i))
    return pl.pallas_call(
        attend_kernel,
        grid_spec=pltpu.PrefetchScalarGridSpec(
            num_scalar_prefetch=1,
            grid=(2,),
            in_specs=[
                head(HEAD_K),
                head(HEAD_K),
                head(VAL),
                head(HEAD_K),
                whole(chunk, 1),
                whole(1, chunk),
                whole(64, ROWS, HEAD_K),
                pl.BlockSpec((1, VAL), lambda i, m: (0, 2 * (m[0] & 1) + i)),
            ],
            out_specs=[
                pl.BlockSpec((rows, VAL), lambda i, m: (0, 2 * (m[0] & 1) + i)),
                pl.BlockSpec((rows, VAL), lambda i, m: (0, i)),
            ],
            scratch_shapes=[
                pltpu.VMEM((chunk, HEAD_K), F32),
                pltpu.VMEM((chunk, HEAD_K), BF16),
                pltpu.VMEM((chunk, VAL), F32),
            ],
        ),
        out_shape=[
            jax.ShapeDtypeStruct((rows, 4 * VAL), BF16),
            jax.ShapeDtypeStruct((rows, 2 * VAL), BF16),
        ],
        cost_estimate=pl.CostEstimate(
            flops=2 * chunk * chunk * 2048, bytes_accessed=6 << 20, transcendentals=0
        ),
        name="attend",
    )(dev, q, k, v, cum, seg_col, seg_row, back, gain)


def finish_kernel(dev, part, other, final, out, final_o, sem):
    width = other.shape[1]
    at = pl.ds(pl.multiple_of((1 - (dev[0] & 1)) * width, width), width)
    copy = pltpu.make_async_copy(other, out.at[:, at], sem)
    copy.start()
    final_o[...] = final[...].astype(F32)
    copy.wait()


def finish(dev, part, other, final):
    vmem, anywhere = pl.BlockSpec(memory_space=pltpu.VMEM), pl.BlockSpec(memory_space=pl.ANY)
    return pl.pallas_call(
        finish_kernel,
        in_specs=[pl.BlockSpec(memory_space=pltpu.SMEM), anywhere, vmem, vmem],
        out_specs=[anywhere, vmem],
        out_shape=[
            jax.ShapeDtypeStruct(part.shape, BF16),
            jax.ShapeDtypeStruct(final.shape, F32),
        ],
        scratch_shapes=[pltpu.SemaphoreType.DMA],
        input_output_aliases={1: 0},
        name="finish",
    )(dev, part, other, final)


def home_route():
    pairs = []
    for t in range(16):
        for p in range(2):
            pairs.append((2 * t + p, 16 * p + 2 * (t % 8) + t // 8))
    return pairs


def exchange(x):
    return lax.all_to_all(x, ("grp", "chip"), split_axis=0, concat_axis=0, tiled=True)


def on_device(
    tokens, w_query, w_key, w_value, w_gate_down, w_gate_up, gate_bias, norm_gain, lengths, owner
):
    dev = lax.axis_index(AXES).astype(jnp.int32).reshape(1)
    chunk = 2 * tokens.shape[0]
    reqs = lengths.shape[0]
    other = lax.ppermute(tokens, "core", [(0, 1), (1, 0)])
    lens = lengths.reshape(1, reqs)
    info, which = plan(chunk, lens, owner.reshape(1, reqs))
    k, v, q, khat, cum, seg_col, seg_row, decay = project(
        dev,
        tokens,
        other,
        w_key,
        w_value,
        w_query,
        w_gate_down.T,
        w_gate_up,
        gate_bias.reshape(1, -1),
        lens,
    )

    def with_slots(slots, info, most, v, khat, seg_col, decay):
        if slots is not None:
            got = exchange(pieces(slots, v, khat, seg_col, decay))
            return exchange(scan_chips(info, got))
        got = exchange(pieces(MORE_SLOTS, v, khat, seg_col, decay))

        def another(state):
            start, held = state
            extra = exchange(pieces(MORE_SLOTS, v, khat, seg_col, decay, start.reshape(1)))
            return start + MORE_SLOTS, scan_chips(info, got, more=(start.reshape(1), extra, held))

        done = scan_chips(info, got, MORE_SLOTS)
        _, done = lax.while_loop(lambda s: s[0] < most, another, (jnp.int32(MORE_SLOTS), done))
        return exchange(done)

    back = lax.switch(
        which[0, 0],
        [functools.partial(with_slots, slots) for slots in (*SLOT_CHOICES, None)],
        info,
        which[0, 1],
        v,
        khat,
        seg_col,
        decay,
    )
    final = lax.ppermute(collect(back), ("chip", "core"), home_route())
    part, theirs = attend(dev, q, k, v, cum, seg_col, seg_row, back, norm_gain.reshape(1, -1))
    swapped = lax.ppermute(theirs, "core", [(0, 1), (1, 0)])
    return tuple(finish(dev, part, swapped, final))


def solution(mesh):
    inner = Mesh(mesh.devices.reshape(4, 16, 2), AXES)
    spread = P(AXES, None)
    return jax.shard_map(
        on_device,
        mesh=inner,
        in_specs=(spread, P(), P(), P(), P(), P(), P(), P(), P(), P()),
        out_specs=(spread, P("grp", ("chip", "core"), None)),
        check_vma=False,
    )
```

```python
import functools

import jax
import jax.numpy as jnp
from jax import lax
from jax.experimental import pallas as pl
from jax.experimental.pallas import tpu as pltpu
from jax.sharding import Mesh
from jax.sharding import PartitionSpec as P

H = 4
HEAD_K = 256
VAL = 512
SPAN = 64
SLOT_CHOICES = (4, 5, 6)
MORE_SLOTS = 4
ROWS = 16
HEAD = 2 * ROWS + 8
F32 = jnp.float32
BF16 = jnp.bfloat16
AXES = ("grp", "chip", "core")
NT = (((1,), (1,)), ((), ()))


def iota(shape, axis):
    return lax.broadcasted_iota(jnp.int32, shape, axis)


def split2(x):
    a = x.astype(BF16)
    return a, (x - a.astype(F32)).astype(BF16)


def split3(x):
    a = x.astype(BF16)
    r = x - a.astype(F32)
    b = r.astype(BF16)
    return a, b, (r - b.astype(F32)).astype(BF16)


def holder_order(inverse):
    row = iota((1, VAL), 1) if inverse else iota((VAL, 1), 0)
    sub = row & 7
    value = 64 * (2 * (sub & 3) + (sub >> 2)) + (row >> 3)
    col = iota((VAL, VAL), 0 if inverse else 1)
    return jnp.where(col == value, 1.0, 0.0).astype(BF16)


def ends_of(lens, down, across):
    lens_f = lens.astype(F32)
    lens_col = jnp.sum(jnp.where(down == across, lens_f, 0.0), axis=1, keepdims=True)
    ends_col = jnp.sum(jnp.where(across <= down, lens_f, 0.0), axis=1, keepdims=True)
    ends_row = jnp.sum(jnp.where(down <= across, lens_col, 0.0), axis=0, keepdims=True)
    return ends_col, ends_row


def plan_kernel(chunk, lens, owner, unused, info_o, which_o):
    reqs = lens.shape[1]
    ends_col, ends = ends_of(lens[...], iota((reqs, reqs), 0), iota((reqs, reqs), 1))
    chip = jnp.floor((ends - 0.5) * (1.0 / chunk))
    seen = jnp.sum(jnp.where(ends_col <= chip * chunk, 1.0, 0.0), axis=0, keepdims=True)
    slot = iota((1, reqs), 1).astype(F32) - seen
    enters = jnp.where(ends - lens[...].astype(F32) < chip * chunk, 1, 0)
    at = iota((1, reqs), 1).astype(F32) * chunk
    first = jnp.sum(jnp.where(ends_col < at, 1.0, 0.0), axis=0, keepdims=True)
    last = jnp.sum(jnp.where(ends_col <= at + (chunk - 1.0), 1.0, 0.0), axis=0, keepdims=True)
    inside = jnp.where(first == last, 1, 0)
    rows = (chip.astype(jnp.int32), slot.astype(jnp.int32), enters, owner[...], inside)
    for n, row in enumerate(rows):
        info_o[n : n + 1, 0:reqs] = row
    most = jnp.max(slot, axis=1, keepdims=True) + 1.0
    which = sum(jnp.where(most > float(slots), 1, 0) for slots in SLOT_CHOICES)
    which_o[...] = jnp.concatenate([which, most.astype(jnp.int32)], axis=1)


def plan(chunk, lens, owner, gain):
    vmem = pl.BlockSpec(memory_space=pltpu.VMEM)
    return pl.pallas_call(
        functools.partial(plan_kernel, chunk),
        in_specs=[vmem] * 2 + [pl.BlockSpec(memory_space=pl.ANY)],
        out_specs=[vmem] * 2,
        out_shape=[
            jax.ShapeDtypeStruct((8, 128), jnp.int32),
            jax.ShapeDtypeStruct((1, 2), jnp.int32),
        ],
        name="plan",
    )(lens, owner, gain)


def here(x):
    return pltpu.with_memory_space_constraint(x, pltpu.VMEM)


def far(x):
    return pltpu.with_memory_space_constraint(x, pltpu.HBM)


def project_kernel(
    dev,
    tok_a,
    tok_b,
    w_k,
    w_v,
    w_q,
    w_down,
    w_up,
    bias,
    lens,
    k_o,
    v_o,
    q_o,
    khat_o,
    cum_o,
    col_o,
    row_o,
    decay_o,
    tok_s,
    erev_s,
    weights_s,
    q_s,
    cum_s,
    sems,
):
    rows = tok_a.shape[0]
    chunk = 2 * rows
    core = dev[0] & 1
    width = 2 * HEAD_K
    reqs = lens.shape[1]
    blocks = chunk // SPAN

    mine = pl.ds(pl.multiple_of(core * rows, rows), rows)
    theirs = pl.ds(pl.multiple_of((1 - core) * rows, rows), rows)
    copy_a = pltpu.make_async_copy(tok_a, tok_s.at[mine, :], sems.at[0])
    copy_b = pltpu.make_async_copy(tok_b, tok_s.at[theirs, :], sems.at[1])
    copy_a.start()
    copy_b.start()
    blocks_in = []
    for source, first, many in ((w_v, 0, 4), (w_q, 4, 2), (w_k, 6, 2)):
        for n in range(many):
            cols = pl.ds(pl.multiple_of((many * core + n) * HEAD_K, HEAD_K), HEAD_K)
            copy = pltpu.make_async_copy(
                source.at[:, cols], weights_s.at[first + n], sems.at[2 + first + n]
            )
            copy.start()
            blocks_in.append(copy)
    base = ((dev[0] >> 1) * chunk).astype(F32)
    ends_col, ends_row = ends_of(lens[...], iota((reqs, reqs), 0), iota((reqs, reqs), 1))
    pos_col = base + iota((chunk, 1), 0).astype(F32)
    pos_row = base + iota((1, chunk), 1).astype(F32)
    seg_col = jnp.sum(jnp.where(ends_row <= pos_col, 1.0, 0.0), axis=1, keepdims=True)
    seg_row = jnp.sum(jnp.where(ends_col <= pos_row, 1.0, 0.0), axis=0, keepdims=True)
    before = jnp.sum(jnp.where(ends_row < base, 1.0, 0.0), axis=1, keepdims=True)
    seg_col, seg_row = seg_col - before, seg_row - before
    col_o[...] = seg_col
    row_o[...] = seg_row
    six = jnp.concatenate([w_down[...]] * 6, axis=0)
    u1, u2, u3 = split3(w_up[...])
    ups = jnp.concatenate([u1, u2, u3, u1, u2, u1], axis=0)
    copy_a.wait()
    copy_b.wait()
    low = lax.dot_general(tok_s[...], six, NT, preferred_element_type=F32)
    l1, l2, l3 = split3(low)
    rank = w_down.shape[0]
    lane = iota(low.shape, 1)
    low = jnp.where(
        lane < 3 * rank,
        l1.astype(F32),
        jnp.where(lane < 5 * rank, l2.astype(F32), l3.astype(F32)),
    ).astype(BF16)
    b_row, b_col = iota((SPAN, SPAN), 0), iota((SPAN, SPAN), 1)
    low_tri = jnp.where(b_row >= b_col, 1.0, 0.0).astype(BF16)
    low_tri = jnp.concatenate([low_tri] * 2, axis=1)

    def gates(b, over):
        at = slice(b * SPAN, (b + 1) * SPAN)
        seg = seg_col[at, :]
        logit = jnp.dot(low[at, :], ups, preferred_element_type=F32) + bias[...]
        gate = (jnp.minimum(logit, 0.0) - jnp.log(1.0 + jnp.exp(-jnp.abs(logit)))) * (1.0 / 16.0)
        pair = jnp.concatenate(split2(gate), axis=0)
        cum_s[at, :] = jnp.dot(low_tri, pair, preferred_element_type=F32)
        later = jnp.where((b_row < b_col) & (seg == seg_row[:, at]), 1.0, 0.0).astype(BF16)
        later = jnp.concatenate([later] * 2, axis=1)
        rest = jnp.dot(later, pair, preferred_element_type=F32)
        top = rest[0:1, :] + gate[0:1, :]
        if over is not None:
            next_seg = seg_col[(b + 1) * SPAN : (b + 1) * SPAN + 1, :]
            rest = rest + jnp.where(seg == next_seg, over, 0.0)
            top = top + jnp.where(seg[0:1, :] == next_seg, over, 0.0)
        erev_s[at, :] = jnp.exp(rest)
        return top

    over = None
    copies_out = []
    for n, copy in enumerate(blocks_in):
        copy.wait()
        got = jnp.dot(tok_s[...], weights_s[n], preferred_element_type=F32).astype(BF16)
        if n < 4:
            v_o[:, n * HEAD_K : (n + 1) * HEAD_K] = got
        elif n < 6:
            q_s[:, (n - 4) * HEAD_K : (n - 3) * HEAD_K] = got
        else:
            cols = slice((n - 6) * HEAD_K, (n - 5) * HEAD_K)
            k_o[:, cols] = got
            khat_o[:, cols] = (got.astype(F32) * erev_s[:, cols]).astype(BF16)
        if n < blocks:
            over = gates(blocks - 1 - n, over)
        if n == 5:
            copies_out = [
                pltpu.make_async_copy(q_s, q_o, sems.at[10]),
                pltpu.make_async_copy(cum_s, cum_o, sems.at[11]),
            ]
            for out in copies_out:
                out.start()
            decay = jnp.exp(over)
            high = decay.astype(BF16).astype(F32)
            eight = iota((8, 128), 0)
            packed = jnp.zeros((8, 128), F32)
            for m, x in enumerate((high, decay - high)):
                for quarter in range(4):
                    lanes = x[:, quarter * 128 : (quarter + 1) * 128]
                    packed = jnp.where(eight == 4 * m + quarter, lanes, packed)
            decay_o[...] = packed
    for out in copies_out:
        out.wait()


def project(dev, tok_a, tok_b, w_key, w_value, w_query, w_down, w_up, bias, lens):
    rows, depth = tok_a.shape
    chunk = 2 * rows
    rank = w_down.shape[0]
    whole = lambda *shape: pl.BlockSpec(shape, lambda i, m: (0,) * len(shape))
    anywhere, vmem = pl.BlockSpec(memory_space=pltpu.HBM), pl.BlockSpec(memory_space=pltpu.VMEM)
    outs = [
        jax.ShapeDtypeStruct((chunk, 2 * HEAD_K), BF16),
        jax.ShapeDtypeStruct((chunk, 2 * VAL), BF16),
        pltpu.HBM((chunk, 2 * HEAD_K), BF16),
        jax.ShapeDtypeStruct((chunk, 2 * HEAD_K), BF16),
        pltpu.HBM((chunk, 2 * HEAD_K), F32),
        jax.ShapeDtypeStruct((chunk, 1), F32),
        jax.ShapeDtypeStruct((1, chunk), F32),
        jax.ShapeDtypeStruct((8, 128), F32),
    ]
    return pl.pallas_call(
        project_kernel,
        grid_spec=pltpu.PrefetchScalarGridSpec(
            num_scalar_prefetch=1,
            grid=(1,),
            in_specs=[
                anywhere,
                vmem,
                anywhere,
                anywhere,
                anywhere,
                whole(rank, depth),
                pl.BlockSpec((rank, 2 * HEAD_K), lambda i, m: (0, m[0] & 1)),
                pl.BlockSpec((1, 2 * HEAD_K), lambda i, m: (0, m[0] & 1)),
                whole(1, lens.shape[1]),
            ],
            out_specs=[vmem, vmem, anywhere, vmem, anywhere, vmem, vmem, vmem],
            scratch_shapes=[
                pltpu.VMEM((chunk, depth), BF16),
                pltpu.VMEM((chunk, 2 * HEAD_K), F32),
                pltpu.VMEM((8, depth, HEAD_K), BF16),
                pltpu.VMEM((chunk, 2 * HEAD_K), BF16),
                pltpu.VMEM((chunk, 2 * HEAD_K), F32),
                pltpu.SemaphoreType.DMA((12,)),
            ],
        ),
        out_shape=outs,
        compiler_params=pltpu.CompilerParams(vmem_limit_bytes=24 << 20),
        cost_estimate=pl.CostEstimate(
            flops=2 * chunk * depth * 2048, bytes_accessed=12 << 20, transcendentals=0
        ),
        name="project",
    )(dev, far(tok_a), here(tok_b), far(w_key), far(w_value), far(w_query), far(w_down), far(w_up), far(bias), far(lens))


def pieces_kernel(slots, start, v_ref, khat_ref, seg_col, decay, out_ref):
    order = holder_order(False)
    seg = seg_col[...]
    first, last = seg[0:1, :], seg[-1:, :]
    turned, keys = [], []
    for h in range(2):
        values = v_ref[:, h * VAL : (h + 1) * VAL]
        turned.append(
            lax.dot_general(order, values, NT, preferred_element_type=F32).astype(BF16)
        )
        keys.append(khat_ref[:, h * HEAD_K : (h + 1) * HEAD_K].astype(F32))

    def write(row, which):
        for h in range(2):
            live = jnp.where(seg == which, keys[h], 0.0).astype(BF16)
            piece = jnp.dot(turned[h], live, preferred_element_type=F32)
            piece = piece.reshape(64, 8, HEAD_K).astype(BF16)
            for n in range(2):
                at = slice(row + ROWS * n + 8 * h, row + ROWS * n + 8 * h + 8)
                out_ref[:, at, :] = piece[:, :, n * 128 : (n + 1) * 128]

    if start is None:
        row = HEAD
        write(0, last)
        out_ref[:, 2 * ROWS : HEAD, :] = jnp.broadcast_to(decay[...].astype(BF16)[None], (64, 8, 128))
    else:
        row = 0
        first = first + start[0].astype(F32)
    for j in range(slots):
        write(row + 2 * ROWS * j, first + float(j))


def first_pieces_kernel(slots, *refs):
    pieces_kernel(slots, None, *refs)


def more_pieces_kernel(slots, start, *refs):
    pieces_kernel(slots, start, *refs)


def pieces(slots, values, khat, seg_col, decay, start=None):
    vmem = pl.BlockSpec(memory_space=pltpu.VMEM)
    rows = 2 * ROWS * slots + (HEAD if start is None else 0)
    kernel = first_pieces_kernel if start is None else more_pieces_kernel
    lead = [] if start is None else [start]
    return pl.pallas_call(
        functools.partial(kernel, slots),
        in_specs=[pl.BlockSpec(memory_space=pltpu.SMEM)] * len(lead) + [vmem] * 4,
        out_specs=vmem,
        out_shape=pltpu.VMEM((64, rows, 128), BF16),
        compiler_params=pltpu.CompilerParams(vmem_limit_bytes=12 << 20),
        name="pieces",
    )(*lead, values, khat, seg_col, decay)


COLLECTOR = (0, 1, 2, 3, 8, 9, 10, 11, 4, 5, 6, 7, 12, 13, 14, 15)


def scan_body(start, slots, row, info, got, ends, old, out_ref, keep_s, fin_s):
    chips = got.shape[0]
    reqs = chips
    each = reqs // 4

    def wide(ref, c, first):
        sides = [ref[c, pl.ds(first + n * ROWS, ROWS), :].astype(F32) for n in range(2)]
        return jnp.concatenate(sides, axis=1)

    def scaled(c, flag, state):
        decay = got[c, 2 * ROWS : HEAD, :].astype(F32) * flag.astype(F32)
        decay = decay[0:4, :] + decay[4:8, :]
        heads = []
        for h in range(2):
            row = jnp.concatenate([decay[2 * h : 2 * h + 1, :], decay[2 * h + 1 : 2 * h + 2, :]], axis=1)
            heads.append(row * state[8 * h : 8 * h + 8, :])
        return jnp.concatenate(heads, axis=0)

    def advance(c, state):
        out_ref[c, 0:ROWS, :] = state.astype(BF16)
        keep_s[c] = state
        return scaled(c, info[4, c], state) + wide(got, c, 0)

    lax.fori_loop(0, chips, advance, jnp.zeros((ROWS, HEAD_K), F32), unroll=8)
    if old is not None:
        for g in range(4):
            for u in range(16):
                at = slice((g * 16 + u) * each, (g * 16 + u + 1) * each)
                held = old[g * 16 + COLLECTOR[u], ROWS : ROWS + each, :].astype(F32)
                for n, side in enumerate(fin_s):
                    side[at, :] = held[:, n * 128 : (n + 1) * 128]

    def place(r, slot):
        chip, owner = info[0, r], info[3, r]
        piece = wide(ends, chip, pl.multiple_of(row + slot * 2 * ROWS, 8))
        done = piece + scaled(chip, info[2, r], keep_s[chip])
        first = (owner // each) * (16 * each) + owner % each
        for n, side in enumerate(fin_s):
            side[pl.ds(first, 16, stride=each), :] = done[:, n * 128 : (n + 1) * 128]

    def finish(r, unused):
        slot = info[1, r] - start
        if slots is None:
            place(r, slot)
        else:

            @pl.when((slot >= 0) & (slot < slots))
            def _():
                place(r, slot)

        return unused

    lax.fori_loop(0, reqs, finish, 0, unroll=8 if slots is None else 1)
    for g in range(4):
        for u in range(16):
            at = slice((g * 16 + u) * each, (g * 16 + u + 1) * each)
            for n, side in enumerate(fin_s):
                cols = slice(n * 128, (n + 1) * 128)
                out_ref[g * 16 + COLLECTOR[u], ROWS : ROWS + each, cols] = side[at, :].astype(BF16)


def scan_kernel(slots, info, got, out_ref, keep_s, *fin_s):
    scan_body(0, slots, HEAD, info, got, got, None, out_ref, keep_s, fin_s)


def scan_more_kernel(start, info, got, ends, old, out_ref, keep_s, *fin_s):
    scan_body(start[0], MORE_SLOTS, 0, info, got, ends, old, out_ref, keep_s, fin_s)


def scan_chips(info, got, slots=None, more=None):
    chips = got.shape[0]
    smem, vmem = pl.BlockSpec(memory_space=pltpu.SMEM), pl.BlockSpec(memory_space=pltpu.VMEM)
    if more is None:
        kernel = functools.partial(scan_kernel, slots)
        args, specs = (info, here(got)), [smem, vmem]
    else:
        start, ends, old = more
        kernel, args = scan_more_kernel, (start, info, got, ends, old)
        specs = [smem, smem, vmem, vmem, vmem]
    return pl.pallas_call(
        kernel,
        in_specs=specs,
        out_specs=vmem,
        out_shape=pltpu.VMEM((chips, ROWS + chips // 4, HEAD_K), BF16),
        compiler_params=pltpu.CompilerParams(vmem_limit_bytes=12 << 20),
        scratch_shapes=[
            pltpu.VMEM((chips, ROWS, HEAD_K), F32),
            pltpu.VMEM((16 * chips, 128), F32),
            pltpu.VMEM((16 * chips, 128), F32),
        ],
        cost_estimate=pl.CostEstimate(flops=1 << 20, bytes_accessed=6 << 20, transcendentals=0),
        name="scan_chips",
    )(*args)


def collect_kernel(back, out_ref, *rows_s):
    reqs = out_ref.shape[0]
    for n, side in enumerate(rows_s):
        cols = slice(n * 128, (n + 1) * 128)
        side[...] = back[:, ROWS : ROWS + reqs, cols].astype(F32).reshape(64 * reqs, 128)
        for j in range(reqs):
            out_ref[j, :, cols] = side[pl.ds(j, 64, stride=reqs), :].astype(BF16)


def collect(back):
    reqs = back.shape[1] - ROWS
    vmem = pl.BlockSpec(memory_space=pltpu.VMEM)
    return pl.pallas_call(
        collect_kernel,
        in_specs=[vmem],
        out_specs=vmem,
        out_shape=pltpu.VMEM((reqs, 64, HEAD_K), BF16),
        scratch_shapes=[pltpu.VMEM((64 * reqs, 128), F32)] * 2,
        compiler_params=pltpu.CompilerParams(vmem_limit_bytes=12 << 20),
        cost_estimate=pl.CostEstimate(flops=1 << 16, bytes_accessed=2 << 20, transcendentals=0),
        name="collect",
    )(here(back))


def attend_kernel(
    dev, q_ref, k_ref, v_ref, cum_ref, seg_col, seg_row, back, gain_ref, mine_o, other_o, *scratch
):
    chunk = q_ref.shape[0]
    rows = chunk // 2
    core = dev[0] & 1
    causal = iota((SPAN, SPAN), 0) >= iota((SPAN, SPAN), 1)
    for h in range(2):
        keys = slice(h * HEAD_K, (h + 1) * HEAD_K)
        vals = slice(h * VAL, (h + 1) * VAL)
        far_s, qin_s, sum_s = scratch[3 * h : 3 * h + 3]
        far_s[...] = jnp.zeros_like(far_s)
        start = jnp.zeros((1, HEAD_K), F32)
        for b in range(chunk // SPAN):
            at = slice(b * SPAN, (b + 1) * SPAN)
            cum = cum_ref[at, keys]
            middle = cum[SPAN // 2 - 1 : SPAN // 2, :]
            last = cum[SPAN - 1 : SPAN, :]
            query = q_ref[at, keys].astype(F32) * (HEAD_K**-0.5)
            entering = query * jnp.exp(cum)
            qin_s[at, :] = jnp.where(seg_col[at, :] == 0.0, entering * jnp.exp(start), 0.0).astype(BF16)
            start = start + last
            key = k_ref[at, keys].astype(F32)
            scores = lax.dot_general(
                (query * jnp.exp(cum - middle)).astype(BF16),
                (key * jnp.exp(middle - cum)).astype(BF16),
                NT,
                preferred_element_type=F32,
            )
            same = seg_col[at, :] == seg_row[:, at]
            near = jnp.where(causal & same, scores, 0.0).astype(BF16)
            total = jnp.dot(near, v_ref[at, vals], preferred_element_type=F32)
            if b > 0:
                reach = 2 * SPAN * ((b + 1) // 2)
                scores = lax.dot_general(
                    entering.astype(BF16),
                    far_s[0:reach, :].astype(BF16),
                    NT,
                    preferred_element_type=F32,
                )
                same = seg_col[at, :] == seg_row[:, 0:reach]
                far = jnp.where(same, scores, 0.0).astype(BF16)
                total += jnp.dot(far, v_ref[0:reach, vals], preferred_element_type=F32)
                far_s[0 : b * SPAN, :] = far_s[0 : b * SPAN, :] * jnp.exp(last)
            far_s[at, :] = key * jnp.exp(last - cum)
            sum_s[at, :] = total
        state = back[:, 8 * h : 8 * h + 8, :].astype(F32)
        state = state.reshape(VAL, HEAD_K).astype(BF16)
        state = jnp.dot(holder_order(True), state, preferred_element_type=F32).astype(BF16)
        wide = pl.ds(pl.multiple_of((2 * core + h) * VAL, VAL), VAL)
        gain = gain_ref[:, wide].astype(F32)
        for side, out in ((1 - core, other_o), (core, mine_o)):
            at = pl.ds(pl.multiple_of(side * rows, rows), rows)
            o = sum_s[at, :] + lax.dot_general(qin_s[at, :], state, NT, preferred_element_type=F32)
            mean = jnp.mean(o * o, axis=1, keepdims=True)
            out[:, vals] = (o * lax.rsqrt(mean + 1e-05) * gain).astype(BF16)


def attend(dev, q, k, v, cum, seg_col, seg_row, back, gain):
    chunk = q.shape[0]
    vmem = pl.BlockSpec(memory_space=pltpu.VMEM)
    half = pltpu.VMEM((chunk // 2, 2 * VAL), BF16)
    return pl.pallas_call(
        attend_kernel,
        in_specs=[pl.BlockSpec(memory_space=pltpu.SMEM)] + [vmem] * 8,
        out_specs=[vmem] * 2,
        out_shape=[half, half],
        scratch_shapes=[
            pltpu.VMEM((chunk, HEAD_K), F32),
            pltpu.VMEM((chunk, HEAD_K), BF16),
            pltpu.VMEM((chunk, VAL), F32),
        ]
        * 2,
        compiler_params=pltpu.CompilerParams(vmem_limit_bytes=12 << 20),
        cost_estimate=pl.CostEstimate(
            flops=2 * chunk * chunk * 2048, bytes_accessed=6 << 20, transcendentals=0
        ),
        name="attend",
    )(dev, far(q), k, v, far(cum), seg_col, seg_row, here(back), gain)


def finish_kernel(dev, mine, other, final, out, final_o, final_s, sems):
    width = other.shape[1]
    core = dev[0] & 1
    copies = []
    for side, half in ((core, mine), (1 - core, other)):
        at = pl.ds(pl.multiple_of(side * width, width), width)
        copies.append(pltpu.make_async_copy(half, out.at[:, at], sems.at[len(copies)]))
        copies[-1].start()
    reqs = final.shape[0]
    for n in range(4):
        at = slice(n * reqs // 4, (n + 1) * reqs // 4)
        final_s[at] = final[at].astype(F32)
        copies.append(pltpu.make_async_copy(final_s.at[at], final_o.at[at], sems.at[len(copies)]))
        copies[-1].start()
    for copy in copies:
        copy.wait()


def finish(dev, mine, other, final):
    vmem, anywhere = pl.BlockSpec(memory_space=pltpu.VMEM), pl.BlockSpec(memory_space=pl.ANY)
    return pl.pallas_call(
        finish_kernel,
        in_specs=[pl.BlockSpec(memory_space=pltpu.SMEM), vmem, vmem, vmem],
        out_specs=[anywhere, anywhere],
        out_shape=[
            jax.ShapeDtypeStruct((mine.shape[0], 2 * mine.shape[1]), BF16),
            jax.ShapeDtypeStruct(final.shape, F32),
        ],
        scratch_shapes=[pltpu.VMEM(final.shape, F32), pltpu.SemaphoreType.DMA((6,))],
        compiler_params=pltpu.CompilerParams(vmem_limit_bytes=12 << 20),
        name="finish",
    )(dev, here(mine), here(other), here(final))


def home_route():
    pairs = []
    for t in range(16):
        for p in range(2):
            pairs.append((2 * t + p, 16 * p + 2 * (t % 8) + t // 8))
    return pairs


def exchange(x):
    return lax.all_to_all(x, ("grp", "chip"), split_axis=0, concat_axis=0, tiled=True)


def on_device(
    tokens, w_query, w_key, w_value, w_gate_down, w_gate_up, gate_bias, norm_gain, lengths, owner
):
    dev = lax.axis_index(AXES).astype(jnp.int32).reshape(1)
    chunk = 2 * tokens.shape[0]
    reqs = lengths.shape[0]
    other = lax.ppermute(tokens, "core", [(0, 1), (1, 0)])
    lens = lengths.reshape(1, reqs)
    gain = norm_gain.reshape(1, -1)
    info, which = plan(chunk, lens, owner.reshape(1, reqs), gain)
    k, v, q, khat, cum, seg_col, seg_row, decay = project(
        dev,
        tokens,
        other,
        w_key,
        w_value,
        w_query,
        w_gate_down.T,
        w_gate_up,
        gate_bias.reshape(1, -1),
        lens,
    )

    def with_slots(slots, info, most, v, khat, seg_col, decay):
        if slots is not None:
            got = exchange(pieces(slots, v, khat, seg_col, decay))
            return exchange(scan_chips(info, got))
        got = exchange(pieces(MORE_SLOTS, v, khat, seg_col, decay))

        def another(state):
            start, held = state
            extra = exchange(pieces(MORE_SLOTS, v, khat, seg_col, decay, start.reshape(1)))
            return start + MORE_SLOTS, scan_chips(info, got, more=(start.reshape(1), extra, held))

        done = scan_chips(info, got, MORE_SLOTS)
        _, done = lax.while_loop(lambda s: s[0] < most, another, (jnp.int32(MORE_SLOTS), done))
        return exchange(done)

    back = lax.switch(
        which[0, 0],
        [functools.partial(with_slots, slots) for slots in (*SLOT_CHOICES, None)],
        info,
        which[0, 1],
        v,
        khat,
        seg_col,
        decay,
    )
    final = lax.ppermute(collect(back), ("chip", "core"), home_route())
    mine, theirs = attend(dev, q, k, v, cum, seg_col, seg_row, back, gain)
    swapped = lax.ppermute(theirs, "core", [(0, 1), (1, 0)])
    return tuple(finish(dev, mine, swapped, final))


def solution(mesh):
    inner = Mesh(mesh.devices.reshape(4, 16, 2), AXES)
    spread = P(AXES, None)
    return jax.shard_map(
        on_device,
        mesh=inner,
        in_specs=(spread, P(), P(), P(), P(), P(), P(), P(), P(), P()),
        out_specs=(spread, P("grp", ("chip", "core"), None)),
        check_vma=False,
    )
```

```python
import functools

import jax
import jax.numpy as jnp
from jax import lax
from jax.experimental import pallas as pl
from jax.experimental.pallas import tpu as pltpu
from jax.sharding import Mesh
from jax.sharding import PartitionSpec as P

H = 4
HEAD_K = 256
VAL = 512
SPAN = 64
SLOT_CHOICES = (4, 5, 6)
MORE_SLOTS = 4
ROWS = 16
HEAD = 2 * ROWS + 8
F32 = jnp.float32
BF16 = jnp.bfloat16
AXES = ("grp", "chip", "core")
NT = (((1,), (1,)), ((), ()))


def iota(shape, axis):
    return lax.broadcasted_iota(jnp.int32, shape, axis)


def split2(x):
    a = x.astype(BF16)
    return a, (x - a.astype(F32)).astype(BF16)


def split3(x):
    a = x.astype(BF16)
    r = x - a.astype(F32)
    b = r.astype(BF16)
    return a, b, (r - b.astype(F32)).astype(BF16)


def holder_order(inverse):
    row = iota((1, VAL), 1) if inverse else iota((VAL, 1), 0)
    sub = row & 7
    value = 64 * (2 * (sub & 3) + (sub >> 2)) + (row >> 3)
    col = iota((VAL, VAL), 0 if inverse else 1)
    return jnp.where(col == value, 1.0, 0.0).astype(BF16)


def ends_of(lens, down, across):
    lens_f = lens.astype(F32)
    lens_col = jnp.sum(jnp.where(down == across, lens_f, 0.0), axis=1, keepdims=True)
    ends_col = jnp.sum(jnp.where(across <= down, lens_f, 0.0), axis=1, keepdims=True)
    ends_row = jnp.sum(jnp.where(down <= across, lens_col, 0.0), axis=0, keepdims=True)
    return ends_col, ends_row


def plan_kernel(chunk, lens, owner, unused, info_o, which_o):
    reqs = lens.shape[1]
    ends_col, ends = ends_of(lens[...], iota((reqs, reqs), 0), iota((reqs, reqs), 1))
    chip = jnp.floor((ends - 0.5) * (1.0 / chunk))
    seen = jnp.sum(jnp.where(ends_col <= chip * chunk, 1.0, 0.0), axis=0, keepdims=True)
    slot = iota((1, reqs), 1).astype(F32) - seen
    enters = jnp.where(ends - lens[...].astype(F32) < chip * chunk, 1, 0)
    at = iota((1, reqs), 1).astype(F32) * chunk
    first = jnp.sum(jnp.where(ends_col < at, 1.0, 0.0), axis=0, keepdims=True)
    last = jnp.sum(jnp.where(ends_col <= at + (chunk - 1.0), 1.0, 0.0), axis=0, keepdims=True)
    inside = jnp.where(first == last, 1, 0)
    rows = (chip.astype(jnp.int32), slot.astype(jnp.int32), enters, owner[...], inside)
    for n, row in enumerate(rows):
        info_o[n : n + 1, 0:reqs] = row
    most = jnp.max(slot, axis=1, keepdims=True) + 1.0
    which = sum(jnp.where(most > float(slots), 1, 0) for slots in SLOT_CHOICES)
    which_o[...] = jnp.concatenate([which, most.astype(jnp.int32)], axis=1)


def plan(chunk, lens, owner, gain):
    vmem = pl.BlockSpec(memory_space=pltpu.VMEM)
    return pl.pallas_call(
        functools.partial(plan_kernel, chunk),
        in_specs=[vmem] * 2 + [pl.BlockSpec(memory_space=pl.ANY)],
        out_specs=[vmem] * 2,
        out_shape=[
            jax.ShapeDtypeStruct((8, 128), jnp.int32),
            jax.ShapeDtypeStruct((1, 2), jnp.int32),
        ],
        name="plan",
    )(lens, owner, gain)


def here(x):
    return pltpu.with_memory_space_constraint(x, pltpu.VMEM)


def far(x):
    return pltpu.with_memory_space_constraint(x, pltpu.HBM)


def project_kernel(
    dev,
    tok_a,
    tok_b,
    w_k,
    w_v,
    w_q,
    down_in,
    up_in,
    bias_in,
    lens_in,
    k_o,
    v_o,
    q_o,
    khat_o,
    cum_o,
    col_o,
    row_o,
    decay_o,
    tok_s,
    erev_s,
    weights_s,
    q_s,
    cum_s,
    w_down,
    w_up,
    bias,
    lens,
    sems,
):
    rows = tok_a.shape[0]
    chunk = 2 * rows
    core = dev[0] & 1
    width = 2 * HEAD_K
    reqs = lens.shape[1]
    blocks = chunk // SPAN

    mine = pl.ds(pl.multiple_of(core * rows, rows), rows)
    theirs = pl.ds(pl.multiple_of((1 - core) * rows, rows), rows)
    copy_a = pltpu.make_async_copy(tok_a, tok_s.at[mine, :], sems.at[0])
    copy_b = pltpu.make_async_copy(tok_b, tok_s.at[theirs, :], sems.at[1])
    half = pl.ds(pl.multiple_of(core * width, width), width)
    small = [
        pltpu.make_async_copy(source, to, sems.at[12 + n])
        for n, (source, to) in enumerate(
            (
                (lens_in, lens),
                (down_in, w_down),
                (up_in.at[:, half], w_up),
                (bias_in.at[:, half], bias),
            )
        )
    ]
    small[0].start()
    copy_a.start()
    copy_b.start()
    for copy in small[1:]:
        copy.start()
    blocks_in = []
    for source, first, many in ((w_v, 0, 4), (w_q, 4, 2), (w_k, 6, 2)):
        for n in range(many):
            cols = pl.ds(pl.multiple_of((many * core + n) * HEAD_K, HEAD_K), HEAD_K)
            copy = pltpu.make_async_copy(
                source.at[:, cols], weights_s.at[first + n], sems.at[2 + first + n]
            )
            copy.start()
            blocks_in.append(copy)
    small[0].wait()
    base = ((dev[0] >> 1) * chunk).astype(F32)
    ends_col, ends_row = ends_of(lens[...], iota((reqs, reqs), 0), iota((reqs, reqs), 1))
    pos_col = base + iota((chunk, 1), 0).astype(F32)
    pos_row = base + iota((1, chunk), 1).astype(F32)
    seg_col = jnp.sum(jnp.where(ends_row <= pos_col, 1.0, 0.0), axis=1, keepdims=True)
    seg_row = jnp.sum(jnp.where(ends_col <= pos_row, 1.0, 0.0), axis=0, keepdims=True)
    before = jnp.sum(jnp.where(ends_row < base, 1.0, 0.0), axis=1, keepdims=True)
    seg_col, seg_row = seg_col - before, seg_row - before
    col_o[...] = seg_col
    row_o[...] = seg_row
    for copy in small[1:]:
        copy.wait()
    six = jnp.concatenate([w_down[...]] * 6, axis=0)
    u1, u2, u3 = split3(w_up[...])
    ups = jnp.concatenate([u1, u2, u3, u1, u2, u1], axis=0)
    copy_a.wait()
    copy_b.wait()
    low = lax.dot_general(tok_s[...], six, NT, preferred_element_type=F32)
    l1, l2, l3 = split3(low)
    rank = w_down.shape[0]
    lane = iota(low.shape, 1)
    low = jnp.where(
        lane < 3 * rank,
        l1.astype(F32),
        jnp.where(lane < 5 * rank, l2.astype(F32), l3.astype(F32)),
    ).astype(BF16)
    b_row, b_col = iota((SPAN, SPAN), 0), iota((SPAN, SPAN), 1)
    low_tri = jnp.where(b_row >= b_col, 1.0, 0.0).astype(BF16)
    low_tri = jnp.concatenate([low_tri] * 2, axis=1)

    def gates(b, over):
        at = slice(b * SPAN, (b + 1) * SPAN)
        seg = seg_col[at, :]
        logit = jnp.dot(low[at, :], ups, preferred_element_type=F32) + bias[...]
        gate = (jnp.minimum(logit, 0.0) - jnp.log(1.0 + jnp.exp(-jnp.abs(logit)))) * (1.0 / 16.0)
        pair = jnp.concatenate(split2(gate), axis=0)
        cum_s[at, :] = jnp.dot(low_tri, pair, preferred_element_type=F32)
        later = jnp.where((b_row < b_col) & (seg == seg_row[:, at]), 1.0, 0.0).astype(BF16)
        later = jnp.concatenate([later] * 2, axis=1)
        rest = jnp.dot(later, pair, preferred_element_type=F32)
        top = rest[0:1, :] + gate[0:1, :]
        if over is not None:
            next_seg = seg_col[(b + 1) * SPAN : (b + 1) * SPAN + 1, :]
            rest = rest + jnp.where(seg == next_seg, over, 0.0)
            top = top + jnp.where(seg[0:1, :] == next_seg, over, 0.0)
        erev_s[at, :] = jnp.exp(rest)
        return top

    over = None
    copies_out = []
    for n, copy in enumerate(blocks_in):
        copy.wait()
        got = jnp.dot(tok_s[...], weights_s[n], preferred_element_type=F32).astype(BF16)
        if n < 4:
            v_o[:, n * HEAD_K : (n + 1) * HEAD_K] = got
        elif n < 6:
            q_s[:, (n - 4) * HEAD_K : (n - 3) * HEAD_K] = got
        else:
            cols = slice((n - 6) * HEAD_K, (n - 5) * HEAD_K)
            k_o[:, cols] = got
            khat_o[:, cols] = (got.astype(F32) * erev_s[:, cols]).astype(BF16)
        if n < blocks:
            over = gates(blocks - 1 - n, over)
        if n == 5:
            copies_out = [
                pltpu.make_async_copy(q_s, q_o, sems.at[10]),
                pltpu.make_async_copy(cum_s, cum_o, sems.at[11]),
            ]
            for out in copies_out:
                out.start()
            decay = jnp.exp(over)
            high = decay.astype(BF16).astype(F32)
            eight = iota((8, 128), 0)
            packed = jnp.zeros((8, 128), F32)
            for m, x in enumerate((high, decay - high)):
                for quarter in range(4):
                    lanes = x[:, quarter * 128 : (quarter + 1) * 128]
                    packed = jnp.where(eight == 4 * m + quarter, lanes, packed)
            decay_o[...] = packed
    for out in copies_out:
        out.wait()


def project(dev, tok_a, tok_b, w_key, w_value, w_query, w_down, w_up, bias, lens):
    rows, depth = tok_a.shape
    chunk = 2 * rows
    rank = w_down.shape[0]
    anywhere, vmem = pl.BlockSpec(memory_space=pltpu.HBM), pl.BlockSpec(memory_space=pltpu.VMEM)
    outs = [
        jax.ShapeDtypeStruct((chunk, 2 * HEAD_K), BF16),
        jax.ShapeDtypeStruct((chunk, 2 * VAL), BF16),
        pltpu.HBM((chunk, 2 * HEAD_K), BF16),
        jax.ShapeDtypeStruct((chunk, 2 * HEAD_K), BF16),
        pltpu.HBM((chunk, 2 * HEAD_K), F32),
        jax.ShapeDtypeStruct((chunk, 1), F32),
        jax.ShapeDtypeStruct((1, chunk), F32),
        jax.ShapeDtypeStruct((8, 128), F32),
    ]
    return pl.pallas_call(
        project_kernel,
        grid_spec=pltpu.PrefetchScalarGridSpec(
            num_scalar_prefetch=1,
            grid=(1,),
            in_specs=[
                anywhere,
                vmem,
                anywhere,
                anywhere,
                anywhere,
                anywhere,
                anywhere,
                anywhere,
                anywhere,
            ],
            out_specs=[vmem, vmem, anywhere, vmem, anywhere, vmem, vmem, vmem],
            scratch_shapes=[
                pltpu.VMEM((chunk, depth), BF16),
                pltpu.VMEM((chunk, 2 * HEAD_K), F32),
                pltpu.VMEM((8, depth, HEAD_K), BF16),
                pltpu.VMEM((chunk, 2 * HEAD_K), BF16),
                pltpu.VMEM((chunk, 2 * HEAD_K), F32),
                pltpu.VMEM((rank, depth), BF16),
                pltpu.VMEM((rank, 2 * HEAD_K), F32),
                pltpu.VMEM((1, 2 * HEAD_K), F32),
                pltpu.VMEM((1, lens.shape[1]), jnp.int32),
                pltpu.SemaphoreType.DMA((16,)),
            ],
        ),
        out_shape=outs,
        compiler_params=pltpu.CompilerParams(vmem_limit_bytes=24 << 20),
        cost_estimate=pl.CostEstimate(
            flops=2 * chunk * depth * 2048, bytes_accessed=12 << 20, transcendentals=0
        ),
        name="project",
    )(dev, far(tok_a), here(tok_b), far(w_key), far(w_value), far(w_query), far(w_down), far(w_up), far(bias), far(lens))


def pieces_kernel(slots, start, v_ref, khat_ref, seg_col, decay, out_ref):
    order = holder_order(False)
    seg = seg_col[...]
    first, last = seg[0:1, :], seg[-1:, :]
    turned, keys = [], []
    for h in range(2):
        values = v_ref[:, h * VAL : (h + 1) * VAL]
        turned.append(
            lax.dot_general(order, values, NT, preferred_element_type=F32).astype(BF16)
        )
        keys.append(khat_ref[:, h * HEAD_K : (h + 1) * HEAD_K].astype(F32))

    def write(row, which):
        for h in range(2):
            live = jnp.where(seg == which, keys[h], 0.0).astype(BF16)
            piece = jnp.dot(turned[h], live, preferred_element_type=F32)
            piece = piece.reshape(64, 8, HEAD_K).astype(BF16)
            for n in range(2):
                at = slice(row + ROWS * n + 8 * h, row + ROWS * n + 8 * h + 8)
                out_ref[:, at, :] = piece[:, :, n * 128 : (n + 1) * 128]

    if start is None:
        row = HEAD
        write(0, last)
        out_ref[:, 2 * ROWS : HEAD, :] = jnp.broadcast_to(decay[...].astype(BF16)[None], (64, 8, 128))
    else:
        row = 0
        first = first + start[0].astype(F32)
    for j in range(slots):
        write(row + 2 * ROWS * j, first + float(j))


def first_pieces_kernel(slots, *refs):
    pieces_kernel(slots, None, *refs)


def more_pieces_kernel(slots, start, *refs):
    pieces_kernel(slots, start, *refs)


def pieces(slots, values, khat, seg_col, decay, start=None):
    vmem = pl.BlockSpec(memory_space=pltpu.VMEM)
    rows = 2 * ROWS * slots + (HEAD if start is None else 0)
    kernel = first_pieces_kernel if start is None else more_pieces_kernel
    lead = [] if start is None else [start]
    return pl.pallas_call(
        functools.partial(kernel, slots),
        in_specs=[pl.BlockSpec(memory_space=pltpu.SMEM)] * len(lead) + [vmem] * 4,
        out_specs=vmem,
        out_shape=pltpu.VMEM((64, rows, 128), BF16),
        compiler_params=pltpu.CompilerParams(vmem_limit_bytes=12 << 20),
        name="pieces",
    )(*lead, values, khat, seg_col, decay)


COLLECTOR = (0, 1, 2, 3, 8, 9, 10, 11, 4, 5, 6, 7, 12, 13, 14, 15)


def scan_body(start, slots, row, info, got, ends, old, out_ref, keep_s, fin_s):
    chips = got.shape[0]
    reqs = chips
    each = reqs // 4

    def wide(ref, c, first):
        sides = [ref[c, pl.ds(first + n * ROWS, ROWS), :].astype(F32) for n in range(2)]
        return jnp.concatenate(sides, axis=1)

    def scaled(c, flag, state):
        decay = got[c, 2 * ROWS : HEAD, :].astype(F32) * flag.astype(F32)
        decay = decay[0:4, :] + decay[4:8, :]
        heads = []
        for h in range(2):
            row = jnp.concatenate([decay[2 * h : 2 * h + 1, :], decay[2 * h + 1 : 2 * h + 2, :]], axis=1)
            heads.append(row * state[8 * h : 8 * h + 8, :])
        return jnp.concatenate(heads, axis=0)

    def advance(c, state):
        out_ref[c, 0:ROWS, :] = state.astype(BF16)
        keep_s[c] = state
        return scaled(c, info[4, c], state) + wide(got, c, 0)

    lax.fori_loop(0, chips, advance, jnp.zeros((ROWS, HEAD_K), F32), unroll=16)
    if old is not None:
        for g in range(4):
            for u in range(16):
                at = slice((g * 16 + u) * each, (g * 16 + u + 1) * each)
                held = old[g * 16 + COLLECTOR[u], ROWS : ROWS + each, :].astype(F32)
                for n, side in enumerate(fin_s):
                    side[at, :] = held[:, n * 128 : (n + 1) * 128]

    def place(r, slot):
        chip, owner = info[0, r], info[3, r]
        piece = wide(ends, chip, pl.multiple_of(row + slot * 2 * ROWS, 8))
        done = piece + scaled(chip, info[2, r], keep_s[chip])
        first = (owner // each) * (16 * each) + owner % each
        for n, side in enumerate(fin_s):
            side[pl.ds(first, 16, stride=each), :] = done[:, n * 128 : (n + 1) * 128]

    def finish(r, unused):
        slot = info[1, r] - start
        if slots is None:
            place(r, slot)
        else:

            @pl.when((slot >= 0) & (slot < slots))
            def _():
                place(r, slot)

        return unused

    lax.fori_loop(0, reqs, finish, 0, unroll=16 if slots is None else 1)
    for g in range(4):
        for u in range(16):
            at = slice((g * 16 + u) * each, (g * 16 + u + 1) * each)
            for n, side in enumerate(fin_s):
                cols = slice(n * 128, (n + 1) * 128)
                out_ref[g * 16 + COLLECTOR[u], ROWS : ROWS + each, cols] = side[at, :].astype(BF16)


def scan_kernel(slots, info, got, out_ref, keep_s, *fin_s):
    scan_body(0, slots, HEAD, info, got, got, None, out_ref, keep_s, fin_s)


def scan_more_kernel(start, info, got, ends, old, out_ref, keep_s, *fin_s):
    scan_body(start[0], MORE_SLOTS, 0, info, got, ends, old, out_ref, keep_s, fin_s)


def scan_chips(info, got, slots=None, more=None):
    chips = got.shape[0]
    smem, vmem = pl.BlockSpec(memory_space=pltpu.SMEM), pl.BlockSpec(memory_space=pltpu.VMEM)
    if more is None:
        kernel = functools.partial(scan_kernel, slots)
        args, specs = (info, here(got)), [smem, vmem]
    else:
        start, ends, old = more
        kernel, args = scan_more_kernel, (start, info, got, ends, old)
        specs = [smem, smem, vmem, vmem, vmem]
    return pl.pallas_call(
        kernel,
        in_specs=specs,
        out_specs=vmem,
        out_shape=pltpu.VMEM((chips, ROWS + chips // 4, HEAD_K), BF16),
        compiler_params=pltpu.CompilerParams(vmem_limit_bytes=12 << 20),
        scratch_shapes=[
            pltpu.VMEM((chips, ROWS, HEAD_K), F32),
            pltpu.VMEM((16 * chips, 128), F32),
            pltpu.VMEM((16 * chips, 128), F32),
        ],
        cost_estimate=pl.CostEstimate(flops=1 << 20, bytes_accessed=6 << 20, transcendentals=0),
        name="scan_chips",
    )(*args)


def collect_kernel(back, out_ref, *rows_s):
    reqs = out_ref.shape[0]
    for n, side in enumerate(rows_s):
        cols = slice(n * 128, (n + 1) * 128)
        side[...] = back[:, ROWS : ROWS + reqs, cols].astype(F32).reshape(64 * reqs, 128)
        for j in range(reqs):
            out_ref[j, :, cols] = side[pl.ds(j, 64, stride=reqs), :].astype(BF16)


def collect(back):
    reqs = back.shape[1] - ROWS
    vmem = pl.BlockSpec(memory_space=pltpu.VMEM)
    return pl.pallas_call(
        collect_kernel,
        in_specs=[vmem],
        out_specs=vmem,
        out_shape=pltpu.VMEM((reqs, 64, HEAD_K), BF16),
        scratch_shapes=[pltpu.VMEM((64 * reqs, 128), F32)] * 2,
        compiler_params=pltpu.CompilerParams(vmem_limit_bytes=12 << 20),
        cost_estimate=pl.CostEstimate(flops=1 << 16, bytes_accessed=2 << 20, transcendentals=0),
        name="collect",
    )(here(back))


def attend_kernel(
    dev, q_ref, k_ref, v_ref, cum_ref, seg_col, seg_row, back, gain_ref, mine_o, other_o, *scratch
):
    chunk = q_ref.shape[0]
    rows = chunk // 2
    core = dev[0] & 1
    causal = iota((SPAN, SPAN), 0) >= iota((SPAN, SPAN), 1)
    starts = [jnp.zeros((1, HEAD_K), F32)] * 2
    for h in range(2):
        scratch[3 * h][...] = jnp.zeros((chunk, HEAD_K), F32)
    for b in range(chunk // SPAN):
        at = slice(b * SPAN, (b + 1) * SPAN)
        reach = 2 * SPAN * ((b + 1) // 2)
        same = seg_col[at, :] == seg_row[:, at]
        for h in range(2):
            keys = slice(h * HEAD_K, (h + 1) * HEAD_K)
            vals = slice(h * VAL, (h + 1) * VAL)
            far_s, qin_s, sum_s = scratch[3 * h : 3 * h + 3]
            cum = cum_ref[at, keys]
            middle = cum[SPAN // 2 - 1 : SPAN // 2, :]
            last = cum[SPAN - 1 : SPAN, :]
            query = q_ref[at, keys].astype(F32) * (HEAD_K**-0.5)
            entering = query * jnp.exp(cum)
            enter = jnp.where(seg_col[at, :] == 0.0, entering * jnp.exp(starts[h]), 0.0)
            qin_s[at, :] = enter.astype(BF16)
            starts[h] = starts[h] + last
            key = k_ref[at, keys].astype(F32)
            scores = lax.dot_general(
                (query * jnp.exp(cum - middle)).astype(BF16),
                (key * jnp.exp(middle - cum)).astype(BF16),
                NT,
                preferred_element_type=F32,
            )
            near = jnp.where(causal & same, scores, 0.0).astype(BF16)
            total = jnp.dot(near, v_ref[at, vals], preferred_element_type=F32)
            if b > 0:
                scores = lax.dot_general(
                    entering.astype(BF16),
                    far_s[0:reach, :].astype(BF16),
                    NT,
                    preferred_element_type=F32,
                )
                reached = seg_col[at, :] == seg_row[:, 0:reach]
                far = jnp.where(reached, scores, 0.0).astype(BF16)
                total += jnp.dot(far, v_ref[0:reach, vals], preferred_element_type=F32)
                far_s[0 : b * SPAN, :] = far_s[0 : b * SPAN, :] * jnp.exp(last)
            far_s[at, :] = key * jnp.exp(last - cum)
            sum_s[at, :] = total
    order = holder_order(True)
    for h in range(2):
        vals = slice(h * VAL, (h + 1) * VAL)
        far_s, qin_s, sum_s = scratch[3 * h : 3 * h + 3]
        state = back[:, 8 * h : 8 * h + 8, :].astype(F32)
        state = state.reshape(VAL, HEAD_K).astype(BF16)
        state = jnp.dot(order, state, preferred_element_type=F32).astype(BF16)
        wide = pl.ds(pl.multiple_of((2 * core + h) * VAL, VAL), VAL)
        gain = gain_ref[:, wide].astype(F32)
        for side, out in ((1 - core, other_o), (core, mine_o)):
            at = pl.ds(pl.multiple_of(side * rows, rows), rows)
            o = sum_s[at, :] + lax.dot_general(qin_s[at, :], state, NT, preferred_element_type=F32)
            mean = jnp.mean(o * o, axis=1, keepdims=True)
            out[:, vals] = (o * lax.rsqrt(mean + 1e-05) * gain).astype(BF16)


def attend(dev, q, k, v, cum, seg_col, seg_row, back, gain):
    chunk = q.shape[0]
    vmem = pl.BlockSpec(memory_space=pltpu.VMEM)
    half = pltpu.VMEM((chunk // 2, 2 * VAL), BF16)
    return pl.pallas_call(
        attend_kernel,
        in_specs=[pl.BlockSpec(memory_space=pltpu.SMEM)] + [vmem] * 8,
        out_specs=[vmem] * 2,
        out_shape=[half, half],
        scratch_shapes=[
            pltpu.VMEM((chunk, HEAD_K), F32),
            pltpu.VMEM((chunk, HEAD_K), BF16),
            pltpu.VMEM((chunk, VAL), F32),
        ]
        * 2,
        compiler_params=pltpu.CompilerParams(vmem_limit_bytes=12 << 20),
        cost_estimate=pl.CostEstimate(
            flops=2 * chunk * chunk * 2048, bytes_accessed=6 << 20, transcendentals=0
        ),
        name="attend",
    )(dev, far(q), k, v, far(cum), seg_col, seg_row, here(back), gain)


def finish_kernel(dev, mine, other, final, out, final_o, final_s, sems):
    width = other.shape[1]
    core = dev[0] & 1
    copies = []
    for side, half in ((core, mine), (1 - core, other)):
        at = pl.ds(pl.multiple_of(side * width, width), width)
        copies.append(pltpu.make_async_copy(half, out.at[:, at], sems.at[len(copies)]))
        copies[-1].start()
    reqs = final.shape[0]
    for n in range(4):
        at = slice(n * reqs // 4, (n + 1) * reqs // 4)
        final_s[at] = final[at].astype(F32)
        copies.append(pltpu.make_async_copy(final_s.at[at], final_o.at[at], sems.at[len(copies)]))
        copies[-1].start()
    for copy in copies:
        copy.wait()


def finish(dev, mine, other, final):
    vmem, anywhere = pl.BlockSpec(memory_space=pltpu.VMEM), pl.BlockSpec(memory_space=pl.ANY)
    return pl.pallas_call(
        finish_kernel,
        in_specs=[pl.BlockSpec(memory_space=pltpu.SMEM), vmem, vmem, vmem],
        out_specs=[anywhere, anywhere],
        out_shape=[
            jax.ShapeDtypeStruct((mine.shape[0], 2 * mine.shape[1]), BF16),
            jax.ShapeDtypeStruct(final.shape, F32),
        ],
        scratch_shapes=[pltpu.VMEM(final.shape, F32), pltpu.SemaphoreType.DMA((6,))],
        compiler_params=pltpu.CompilerParams(vmem_limit_bytes=12 << 20),
        name="finish",
    )(dev, here(mine), here(other), here(final))


def home_route():
    pairs = []
    for t in range(16):
        for p in range(2):
            pairs.append((2 * t + p, 16 * p + 2 * (t % 8) + t // 8))
    return pairs


def exchange(x):
    return lax.all_to_all(x, ("grp", "chip"), split_axis=0, concat_axis=0, tiled=True)


def on_device(
    tokens, w_query, w_key, w_value, w_gate_down, w_gate_up, gate_bias, norm_gain, lengths, owner
):
    dev = lax.axis_index(AXES).astype(jnp.int32).reshape(1)
    chunk = 2 * tokens.shape[0]
    reqs = lengths.shape[0]
    other = lax.ppermute(tokens, "core", [(0, 1), (1, 0)])
    lens = lengths.reshape(1, reqs)
    gain = norm_gain.reshape(1, -1)
    info, which = plan(chunk, lens, owner.reshape(1, reqs), gain)
    k, v, q, khat, cum, seg_col, seg_row, decay = project(
        dev,
        tokens,
        other,
        w_key,
        w_value,
        w_query,
        w_gate_down.T,
        w_gate_up,
        gate_bias.reshape(1, -1),
        lens,
    )

    def with_slots(slots, info, most, v, khat, seg_col, decay):
        if slots is not None:
            got = exchange(pieces(slots, v, khat, seg_col, decay))
            return exchange(scan_chips(info, got))
        got = exchange(pieces(MORE_SLOTS, v, khat, seg_col, decay))

        def another(state):
            start, held = state
            extra = exchange(pieces(MORE_SLOTS, v, khat, seg_col, decay, start.reshape(1)))
            return start + MORE_SLOTS, scan_chips(info, got, more=(start.reshape(1), extra, held))

        done = scan_chips(info, got, MORE_SLOTS)
        _, done = lax.while_loop(lambda s: s[0] < most, another, (jnp.int32(MORE_SLOTS), done))
        return exchange(done)

    back = lax.switch(
        which[0, 0],
        [functools.partial(with_slots, slots) for slots in (*SLOT_CHOICES, None)],
        info,
        which[0, 1],
        v,
        khat,
        seg_col,
        decay,
    )
    final = lax.ppermute(collect(back), ("chip", "core"), home_route())
    mine, theirs = attend(dev, q, k, v, cum, seg_col, seg_row, back, gain)
    swapped = lax.ppermute(theirs, "core", [(0, 1), (1, 0)])
    return tuple(finish(dev, mine, swapped, final))


def solution(mesh):
    inner = Mesh(mesh.devices.reshape(4, 16, 2), AXES)
    spread = P(AXES, None)
    return jax.shard_map(
        on_device,
        mesh=inner,
        in_specs=(spread, P(), P(), P(), P(), P(), P(), P(), P(), P()),
        out_specs=(spread, P("grp", ("chip", "core"), None)),
        check_vma=False,
    )
```
